32 devices in a mesh: dp: 8 (over z, y), expert: 4 (over x, core).
Axes of the slice: x: 2, y: 2, z: 4, core: 2. Of those that a mesh axis runs over, the one named last changes fastest.
Arguments:
- tokens_in: bfloat16 [25216, 512], P(('dp', 'expert')), may hold values from -6 to 6
- grad_out: bfloat16 [25216, 512], P(('dp', 'expert')), may hold values from -6 to 6
- routes: int32 [25216, 2], P(('dp', 'expert')), may hold values from 0 to 15, all different within a row; in each aligned block of 197 rows (0 to 196, 197 to 393, ...) at most 41 rows name the same one
- norm_gains: bfloat16 [512, 2], P(('dp', 'expert')), may hold values from 0.5 to 1.5
- biases: bfloat16 [512, 5], P(('dp', 'expert')), may hold values from -1 to 1
- w_qkv: bfloat16 [512, 1536], P(('dp', 'expert')), may hold values from -0.25 to 0.25
- w_proj: bfloat16 [512, 512], P(('dp', 'expert')), may hold values from -2 to 2
- w_router: bfloat16 [512, 16], P(('dp', 'expert')), may hold values from -0.25 to 0.25
- w_up: bfloat16 [16, 512, 2048], P('expert'), may hold values from -0.25 to 0.25
- b_up: bfloat16 [16, 2048], P('expert'), may hold values from -1 to 1
- w_down: bfloat16 [16, 2048, 512], P('expert'), may hold values from -1.5 to 1.5
- b_down: bfloat16 [16, 512], P('expert'), may hold values from -9.5625 to 9.5625
Outputs:
- block_out: bfloat16 [25216, 512], P(('dp', 'expert'))
- grad_tokens: float32 [25216, 512], P(('dp', 'expert'))
- grad_gains: float32 [512, 2], P(('dp', 'expert'))
- grad_biases: float32 [512, 5], P(('dp', 'expert'))
- grad_qkv: float32 [512, 1536], P(('dp', 'expert'))
- grad_proj: float32 [512, 512], P(('dp', 'expert'))
- grad_router: float32 [512, 16], P(('dp', 'expert'))
- grad_up: float32 [16, 512, 2048], P('expert', None, 'dp')
- grad_b_up: float32 [16, 2048], P('expert', 'dp')
- grad_down: float32 [16, 2048, 512], P('expert', 'dp')
- grad_b_down: float32 [16, 512], P('expert', 'dp')
The draws below stay inside these ranges and needn't reach their ends.
Inputs may be any that keep to these rules, and one draw needn't show every extreme that they name: `routes`: each row names two different experts. In each aligned block of 197 rows (one micro-batch of one device) no expert is named by more than 41 rows, and in every draw some expert is named by exactly 41 rows of some block.
All inputs are finite; a program needn't handle non-finite values.
Results may differ from the reference program's by a relative error of at most 0.017.
Values may be sent and summed in bfloat16 or wider, within the bound.
No kernel may reach another device: no remote copies, remote signals or barrier semaphores. Data moves between devices by JAX's collectives and lax.ppermute only.
A program may use at most 256 MiB of HBM per device.

```python
import math
import jax
import jax.numpy as jnp
import numpy as np
from jax import lax

D = 512
HEADS = 8
HEAD = 64
H = 2048
SEQ = 197
IMG_MB = 1
EXPERTS = 16
TOK_MB = 197
TOKENS = 25216
CAP = 41


def strengthened(values, own_key, source, target, shards_of, factor):
    def block_of(dim):
        return (jnp.arange(values.shape[dim]) // (values.shape[dim] // shards_of)).reshape((-1,) + (1,) * (values.ndim - 1 - dim))

    one_side = jax.random.permutation(own_key, shards_of)[block_of(target)]
    far = (block_of(target) + shards_of // 2) % shards_of
    return jnp.where((block_of(source) == one_side) | (block_of(source) == far), factor * values, values)


def level_of(stream_key, extent, cuts, low, top_value):
    loudness = 1.0
    for dim, blocks in cuts:
        draws = jax.random.uniform(jax.random.fold_in(jax.random.fold_in(stream_key, 6), dim), (blocks,), jnp.float32, low / len(cuts), top_value / len(cuts))
        loudness = loudness * jnp.repeat(jnp.exp(draws), extent[dim] // blocks).reshape((-1,) + (1,) * (len(extent) - 1 - dim))
    return loudness


def assign_block(own_key, own, number, rows, count, top, limit, lean):
    sequence = jax.random.permutation(own_key, count)
    heavy_load, common = shares(count, rows * top, limit, lean, True), shares(count, rows * top, limit, lean, False)
    places = jnp.arange(count)

    def named(lengths, rotation):
        used = int((lengths > 0).sum())
        fixed = max(1, used // 4)
        passed = fixed + (places - fixed + rotation * (used - fixed)) % max(1, count - fixed)
        return jnp.zeros((count,), jnp.int32).at[sequence[jnp.where(places < fixed, places, passed)]].set(jnp.asarray(lengths, jnp.int32))

    lengths = jnp.where(number % 4 == 0, named(heavy_load, number // 4), named(common, number - number // 4 - 1))
    mixed = jax.random.permutation(jax.random.fold_in(own, 3), count)
    source_of, sink = mixed[0:count // 2 * 2:2], mixed[1:count // 2 * 2:2]
    slack = jnp.minimum(lengths[source_of] - 1, limit - lengths[sink]) // 2
    slack = jnp.where((source_of == sequence[0]) | (sink == sequence[0]) | (lengths[sink] == 0), 0, jnp.maximum(slack, 0))
    passed = jax.random.randint(jax.random.fold_in(own, 4), (count // 2,), 0, 1 << 20) % (slack + 1)
    lengths = lengths.at[source_of].add(-passed).at[sink].add(passed)
    items = jnp.searchsorted(jnp.cumsum(lengths), jnp.arange(rows * top), side="right").astype(jnp.int32)
    table = items.reshape(top, rows).T
    table = table[jax.random.permutation(jax.random.fold_in(own, 1), rows)]
    rotation = jax.random.randint(jax.random.fold_in(own, 2), (rows, 1), 0, top)
    return jnp.take_along_axis(table, (jnp.arange(top)[None, :] + rotation) % top, axis=1)


def shares(number_of, total, limit, skew, full):
    weights = [(1 << 20) // math.isqrt(rank ** skew) + 1 for rank in range(1, number_of + 1)]
    largest = limit if full else min(limit, max(-(-total // number_of), total * weights[0] // sum(weights)))
    least = 1 if total - largest >= number_of - 1 else 0
    holding, rest = [largest] + [least] * (number_of - 1), total - largest - least * (number_of - 1)
    while rest > 0:
        free = [i for i in range(1, number_of) if holding[i] < largest] or [i for i in range(1, number_of) if holding[i] < limit]
        pool, budget = sum([weights[i] for i in free]), rest
        for i in free:
            extra = min(limit - holding[i], max(1, budget * weights[i] // pool), rest)
            holding[i] = holding[i] + extra
            rest = rest - extra
    return np.array(holding)


def normal_values(stream_key, shape, scale, limit, shards=(), held_as=jnp.bfloat16):
    values = scale * jax.random.normal(stream_key, shape, jnp.float32)
    if shards:
        values = values * level_of(stream_key, shape, shards, -0.22, 0.18)
    return jnp.clip(values, -limit, limit).astype(held_as)


def heavy_noise(own_key, extent, scale, bound, pieces, heavy, kind=jnp.bfloat16):
    drawn = scale * jax.random.normal(own_key, extent, jnp.float32)
    if pieces:
        drawn = drawn * level_of(own_key, extent, pieces, -0.22, 0.18)
    return jnp.clip(strengthened(drawn, jax.random.fold_in(own_key, 3), *heavy), -bound, bound).astype(kind)


def setup_inputs(seed: int = 0) -> dict:
    key_list = jax.random.split(jax.random.key(seed), 13)
    tokens_in = heavy_noise(key_list[0], (TOKENS, D), 1.0, 6.0, ((0, 32),), (0, 1, 32, 2.75))
    grad_out = heavy_noise(key_list[1], (TOKENS, D), 1.0, 6.0, ((0, 32),), (0, 1, 32, 2.75))
    routes_keys = jax.random.split(jax.random.fold_in(key_list[2], 1), TOKENS // TOK_MB)
    routes_turns = jax.random.permutation(jax.random.fold_in(key_list[2], 3), TOKENS // TOK_MB)
    routes = jax.vmap(lambda own, number: assign_block(jax.random.fold_in(key_list[2], 2), own, number, TOK_MB, EXPERTS, 2, CAP, 1))(routes_keys, routes_turns).reshape((TOKENS, 2))
    norm_gains = jnp.clip(1.0 + 0.1 * jax.random.normal(key_list[3], (D, 2), jnp.float32), 0.5, 1.5).astype(jnp.bfloat16)
    biases = normal_values(key_list[4], (D, 5), 0.2, 1.0, ((0, 32),))
    w_qkv = normal_values(key_list[5], (D, 3 * D), D ** -0.5, 0.25, ((0, 32),))
    w_proj = normal_values(key_list[6], (D, D), (D // 64) ** -0.5, 2.0, ((0, 32),))
    w_router = normal_values(key_list[7], (D, EXPERTS), D ** -0.5, 0.25, ((0, 32),))
    w_up = normal_values(key_list[8], (EXPERTS, D, H), D ** -0.5, 0.25, ((0, 4),))
    b_up = normal_values(key_list[9], (EXPERTS, H), 0.2, 1.0, ((0, 4),))
    w_down = normal_values(key_list[10], (EXPERTS, H, D), (max(1, 2 * H // (EXPERTS * EXPERTS))) ** -0.5, 1.5, ((0, 4),))
    b_down = normal_values(key_list[11], (EXPERTS, D), (0.1 * EXPERTS), 9.5625, ((0, 4),))
    return {"tokens_in": tokens_in, "grad_out": grad_out, "routes": routes, "norm_gains": norm_gains, "biases": biases, "w_qkv": w_qkv, "w_proj": w_proj, "w_router": w_router, "w_up": w_up, "b_up": b_up, "w_down": w_down, "b_down": b_down}


@jax.custom_vjp
def low(v):
    return lax.optimization_barrier(v.astype(jnp.bfloat16)).astype(jnp.float32)

@jax.custom_vjp
def low_back(v):
    return v

def low_keep(v):
    return (low(v), None)

def low_pass(kept, grad):
    return (grad,)

def back_keep(v):
    return (v, None)

def back_low(kept, grad):
    return (low(grad),)
low.defvjp(low_keep, low_pass)
low_back.defvjp(back_keep, back_low)
EPSILON = 1e-06
PRECISE = lax.Precision.HIGHEST

def layer_norm(row_block, gain_vec, shift_vec):
    row_mean = lax.optimization_barrier(jnp.mean(row_block, axis=-1, keepdims=True))
    centred = row_block - row_mean
    inv_std = lax.rsqrt(lax.optimization_barrier(jnp.mean(centred * centred, axis=-1, keepdims=True)) + EPSILON)
    return centred * inv_std * gain_vec + shift_vec

def take_rows(source_rows, index_rows):
    return jnp.take(source_rows, index_rows, axis=0)

def attention_block(row_block, norm_gains, biases, w_qkv, w_proj):
    act_one = low(layer_norm(row_block, norm_gains[:, 0], biases[:, 3]))
    qkv_bias = jnp.concatenate([biases[:, 0], jnp.zeros_like(biases[:, 0]), biases[:, 1]])
    qkv_rows = low(low_back(jnp.dot(act_one, w_qkv, precision=PRECISE) + qkv_bias))
    head_parts = qkv_rows.reshape(IMG_MB, SEQ, 3, HEADS, HEAD)
    queries = head_parts[:, :, 0]
    key_rows = head_parts[:, :, 1]
    values = head_parts[:, :, 2]
    scores = low_back(jnp.einsum('ishd,ithd->ihst', queries, key_rows, precision=PRECISE) * HEAD ** (-0.5))
    weights = low(jax.nn.softmax(scores, axis=-1))
    mixed_rows = jnp.einsum('ihst,ithd->ishd', weights, values, precision=PRECISE).reshape(TOK_MB, D)
    mixed_rows = low(low_back(mixed_rows))
    attn_out = low_back(jnp.dot(mixed_rows, w_proj, precision=PRECISE) + biases[:, 2])
    return row_block + attn_out

def expert_apply(packed):
    expert_rows, up_weight, up_bias, down_weight, down_bias = packed
    pre_act = low_back(jnp.dot(expert_rows, up_weight, precision=PRECISE) + up_bias)
    hidden_act = low(jax.nn.gelu(pre_act, approximate=False))
    return jnp.dot(hidden_act, down_weight, precision=PRECISE) + down_bias

def dispatch_tables(routes_blk):
    block_count = routes_blk.shape[0]
    expert_ids = jnp.concatenate([routes_blk[:, :, 0], routes_blk[:, :, 1]], axis=1).astype(jnp.int32)
    chosen = (expert_ids[:, :, None] == jnp.arange(EXPERTS, dtype=jnp.int32)[None, None, :]).astype(jnp.int32)
    running = (jnp.cumsum(chosen, axis=1) - 1).astype(jnp.int32)
    position = lax.optimization_barrier(jnp.sum(chosen * running, axis=2)).astype(jnp.int32)
    slot_of = (expert_ids * CAP + position).astype(jnp.int32)
    slot_table = jnp.full((block_count, EXPERTS * CAP), 2 * TOK_MB, jnp.int32)
    block_idx = jnp.arange(block_count, dtype=jnp.int32)[:, None]
    pair_idx = jnp.broadcast_to(jnp.arange(2 * TOK_MB, dtype=jnp.int32)[None, :], slot_of.shape)
    slot_table = slot_table.at[block_idx, slot_of].set(pair_idx)
    return (slot_of, slot_table)

def forward(tokens_in, norm_gains, biases, w_qkv, w_proj, w_router, w_up, b_up, w_down, b_down, routes_blk, slot_of, slot_table):
    block_rows = tokens_in.reshape(-1, TOK_MB, D)
    block_count = block_rows.shape[0]

    def attend_one(row_block):
        return attention_block(row_block, norm_gains, biases, w_qkv, w_proj)
    resid_one = lax.map(jax.checkpoint(attend_one), block_rows)
    act_two = low(layer_norm(resid_one, norm_gains[:, 1], biases[:, 4]))
    logits = low_back(jnp.einsum('bnd,de->bne', act_two, w_router, precision=PRECISE))
    router_probs = jax.nn.softmax(logits, axis=-1)
    gate_vals = jnp.take_along_axis(router_probs, routes_blk, axis=2)
    rows_two = low_back(jnp.concatenate([act_two, act_two], axis=1))
    padded = jnp.concatenate([rows_two, jnp.zeros((block_count, 1, D), jnp.float32)], axis=1)
    expert_in = jax.vmap(take_rows)(padded, slot_table)
    expert_in = expert_in.reshape(block_count, EXPERTS, CAP, D).transpose(1, 0, 2, 3).reshape(EXPERTS, block_count * CAP, D)
    results = lax.map(jax.checkpoint(expert_apply), (expert_in, w_up, b_up, w_down, b_down))
    results = low(low_back(results))
    results = results.reshape(EXPERTS, block_count, CAP, D).transpose(1, 0, 2, 3).reshape(block_count, EXPERTS * CAP, D)
    picked = jax.vmap(take_rows)(results, slot_of)
    moe_out = gate_vals[:, :, 0:1] * picked[:, :TOK_MB] + gate_vals[:, :, 1:2] * picked[:, TOK_MB:]
    return (resid_one + moe_out).reshape(-1, D)

def reference(tokens_in, grad_out, routes, norm_gains, biases, w_qkv, w_proj, w_router, w_up, b_up, w_down, b_down):
    routes_blk = routes.reshape(-1, TOK_MB, 2).astype(jnp.int32)
    slot_of, slot_table = dispatch_tables(routes_blk)

    def whole_layer(tok_f, gain_f, bias_f, qkv_f, proj_f, router_f, up_f, b_up_f, down_f, b_down_f):
        return forward(tok_f, gain_f, bias_f, qkv_f, proj_f, router_f, up_f, b_up_f, down_f, b_down_f, routes_blk, slot_of, slot_table)
    primals = [tokens_in, norm_gains, biases, w_qkv, w_proj, w_router, w_up, b_up, w_down, b_down]
    primals = [entry.astype(jnp.float32) for entry in primals]
    result, pullback = jax.vjp(whole_layer, *primals)
    grads = pullback(grad_out.astype(jnp.float32))
    return (result.astype(jnp.bfloat16), grads[0], grads[1], grads[2], grads[3], grads[4], grads[5], grads[6], grads[7], grads[8], grads[9])
```

```python
import jax
import jax.numpy as jnp
from jax import lax
from jax.sharding import PartitionSpec as P

HEAD = 64
SEQ = 197
ROWS = 208
MICRO = 4
CORES = 2
EPSILON = 1e-06
BF = jnp.bfloat16
F32 = jnp.float32


def norm_rows(row_block):
    row_mean = jnp.mean(row_block, axis=-1, keepdims=True)
    centred = row_block - row_mean
    inv_std = lax.rsqrt(jnp.mean(centred * centred, axis=-1, keepdims=True) + EPSILON)
    return (centred * inv_std, inv_std)


def norm_back(grad_h, normed, inv_std, gain_vec):
    scaled = grad_h * gain_vec
    return inv_std * (
        scaled
        - jnp.mean(scaled, axis=-1, keepdims=True)
        - normed * jnp.mean(scaled * normed, axis=-1, keepdims=True)
    )


def gelu_parts(pre_act):
    normal_cdf = 0.5 * (1.0 + lax.erf(pre_act * 0.7071067811865476))
    normal_pdf = jnp.exp(-0.5 * pre_act * pre_act) * 0.3989422804014327
    return (normal_cdf, normal_pdf)


def ein(spec, left, right):
    return jnp.einsum(spec, left, right, preferred_element_type=F32)


class Place:
    def __init__(self, mesh):
        self.ne = mesh.shape["expert"]
        self.nd = mesh.shape["dp"]
        self.nx = self.ne // CORES
        bits = self.nd.bit_length() - 1
        self.ny = 1 << (bits // 2)
        self.nz = self.nd // self.ny
        self.nh = self.nz // 2

    def here(self):
        ei = lax.axis_index("expert")
        di = lax.axis_index("dp")
        self.ei, self.di = ei, di
        self.x, self.c = ei // CORES, ei % CORES
        self.z, self.y = di // self.ny, di % self.ny
        self.zh, self.zl = self.z // 2, self.z % 2

    def core(self, val):
        return lax.ppermute(val, "expert", [(i, i ^ 1) for i in range(self.ne)])

    def xs(self, val, k):
        n, c = self.nx, CORES
        return lax.ppermute(val, "expert", [(i, (i // c + k) % n * c + i % c) for i in range(self.ne)])

    def ys(self, val, k):
        n = self.ny
        return lax.ppermute(val, "dp", [(i, i // n * n + (i + k) % n) for i in range(self.nd)])

    def zs(self, val, k):
        n, m = self.nz, self.ny
        return lax.ppermute(val, "dp", [(i, (i // m + k) % n * m + i % m) for i in range(self.nd)])

    def zp(self, val):
        n, m = self.nz, self.ny
        return lax.ppermute(val, "dp", [(i, (i // m ^ 1) * m + i % m) for i in range(self.nd)])

    def zhs(self, val, k):
        n, m = self.nh, self.ny
        return lax.ppermute(
            val,
            "dp",
            [(i, ((i // m // 2 + k) % n * 2 + i // m % 2) * m + i % m) for i in range(self.nd)],
        )

    def group(self, val):
        mine = [val] + [self.xs(val, k) for k in range(1, self.nx)]
        other = [self.core(v) for v in mine]
        return [v for pair in zip(mine, other) for v in pair]


def ordered(parts, own):
    n = len(parts)
    if n == 1:
        return parts[0][None]
    line = jnp.stack(parts[::-1] + parts[::-1])
    return lax.dynamic_slice_in_dim(line, n - 1 - own, n, axis=0)


def gather_dense(pl, piece):
    rows, cols = piece.shape
    val = ordered([piece] + [pl.zs(piece, k) for k in range(1, pl.nz)], pl.z)
    ys = [val] + [pl.ys(val, k) for k in range(1, pl.ny)]
    val = ordered(ys, pl.y)
    xs = [val] + [pl.xs(val, k) for k in range(1, pl.nx)]
    val = ordered(xs, pl.x)
    val = ordered([val, pl.core(val)], pl.c)
    return val.transpose(3, 2, 1, 0, 4, 5).reshape(pl.nd * pl.ne * rows, cols)


def scatter_rows(pl, full):
    cols = full.shape[1]
    val = full.reshape(pl.nz, pl.ny, pl.nx, CORES, -1, cols)

    def pick(v, axis, idx):
        return lax.dynamic_index_in_dim(v, idx, axis, keepdims=False)

    val = pick(val, 3, pl.c) + pl.core(pick(val, 3, pl.c ^ 1).astype(BF)).astype(F32)
    val = pick(val, 2, pl.x) + sum(
        pl.xs(pick(val, 2, (pl.x + k) % pl.nx).astype(BF), k).astype(F32) for k in range(1, pl.nx)
    )
    val = pick(val, 1, pl.y) + sum(
        pl.ys(pick(val, 1, (pl.y + k) % pl.ny).astype(BF), k).astype(F32) for k in range(1, pl.ny)
    )
    val = pick(val, 0, pl.z) + sum(
        pl.zs(pick(val, 0, (pl.z + k) % pl.nz).astype(BF), k).astype(F32) for k in range(1, pl.nz)
    )
    return val


def on_device(
    pl,
    tokens_in,
    grad_out,
    routes,
    norm_gains,
    biases,
    w_qkv,
    w_proj,
    w_router,
    w_up,
    b_up,
    w_down,
    b_down,
):
    pl.here()
    width = tokens_in.shape[1]
    heads = width // HEAD
    local = w_up.shape[0]
    hidden = w_up.shape[2]
    experts = local * pl.ne
    blocks = MICRO
    cap = max(2, (2 * SEQ * 13 + 8 * experts - 1) // (8 * experts))
    slots = -(-cap // 16) * 16
    hb = hidden // pl.nd
    score_scale = HEAD ** (-0.5)
    wide = experts + 7

    tok = tokens_in.reshape(blocks, SEQ, width).astype(F32)
    dy = grad_out.reshape(blocks, SEQ, width)
    pad_rows = lambda v: jnp.pad(v, ((0, 0), (0, ROWS - SEQ), (0, 0)))

    piece = jnp.concatenate([w_qkv, w_proj, w_router, norm_gains, biases], axis=1)
    cols = piece.shape[1]
    piece = jnp.pad(piece, ((0, 0), (0, -cols % 128)))
    dense = gather_dense(pl, piece)
    full_qkv = dense[:, : 3 * width]
    full_proj = dense[:, 3 * width : 4 * width]
    full_router = dense[:, 4 * width : 4 * width + experts]
    vecs = dense[:, 4 * width + experts : 4 * width + wide].astype(F32)
    gain_one, gain_two = vecs[:, 0], vecs[:, 1]
    bias_q, bias_v, bias_p, shift_one, shift_two = [vecs[:, 2 + i] for i in range(5)]

    route_rows = routes.reshape(blocks, SEQ, 2)
    names = jnp.arange(experts, dtype=jnp.int32)
    onehot = [(route_rows[:, :, c, None] == names).astype(F32) for c in range(2)]
    sel = onehot[0] + onehot[1]
    tri = (jnp.arange(SEQ)[:, None] >= jnp.arange(SEQ)[None, :]).astype(BF)
    pos = ein("ts,bse->bet", tri, sel.astype(BF)).astype(jnp.int32) - 1
    pos = jnp.where(sel.transpose(0, 2, 1) > 0, pos, -1)
    pos = jnp.pad(pos, ((0, 0), (0, 0), (0, ROWS - SEQ)), constant_values=-1)

    normed_one, inv_one = norm_rows(tok)
    act_one = (normed_one * gain_one + shift_one).astype(BF)
    qkv_bias = jnp.concatenate([bias_q, jnp.zeros_like(bias_q), bias_v])
    qkv = (ein("btd,df->btf", act_one, full_qkv) + qkv_bias).astype(BF)
    parts = qkv.reshape(blocks, SEQ, 3, heads, HEAD)
    queries, keys, values = parts[:, :, 0], parts[:, :, 1], parts[:, :, 2]
    scores = ein("ishd,ithd->ihst", queries, keys) * score_scale
    top = jnp.max(scores, axis=-1, keepdims=True)
    lse = top + jnp.log(jnp.sum(jnp.exp(scores - top), axis=-1, keepdims=True))
    probs = jnp.exp(scores - lse)
    mixed = ein("ihst,ithd->ishd", probs.astype(BF), values).astype(BF).reshape(blocks, SEQ, width)
    resid = tok + ein("btd,df->btf", mixed, full_proj) + bias_p
    normed_two, inv_two = norm_rows(resid)
    act_two = (normed_two * gain_two + shift_two).astype(BF)
    router = jax.nn.softmax(ein("btd,de->bte", act_two, full_router), axis=-1)

    act_pad, dy_pad = pad_rows(act_two), pad_rows(dy)
    mine = [act_pad, dy_pad, pos]
    peer = [pl.zp(v) for v in mine]
    near = list(zip(*[pl.group(v) for v in mine]))
    far = list(zip(*[pl.group(v) for v in peer]))

    def gather(source):
        act, dys, where = source
        logits = ein("btd,de->bte", act, full_router)
        gates = jax.nn.softmax(logits, axis=-1)
        own = lax.dynamic_slice_in_dim(where, pl.ei * local, local, axis=1)
        gates = lax.dynamic_slice_in_dim(gates, pl.ei * local, local, axis=2)
        pick = jnp.arange(slots)[None, None, :, None] == own[:, :, None, :]
        pickb = pick.astype(BF)
        rows = ein("bejt,btd->ebjd", pickb, act).astype(BF)
        dyr = ein("bejt,btd->ebjd", pickb, dys).astype(BF)
        gate = jnp.sum(jnp.where(pick, gates.transpose(0, 2, 1)[:, :, None, :], 0.0), axis=3)
        gate = gate.transpose(1, 0, 2)
        flat = lambda v: v.reshape(local, blocks * slots, *v.shape[3:])
        return flat(rows), flat(dyr), flat(gate), pickb

    near_g = [gather(s) for s in near]
    far_g = [gather(s) for s in far]
    cat = lambda gs, i: jnp.concatenate([g[i] for g in gs], axis=1)
    b_up_f, b_down_f = b_up.astype(F32), b_down.astype(F32)

    rows, dyr, gate = [cat(near_g, i) for i in range(3)]
    dres = (gate[:, :, None] * dyr.astype(F32)).astype(BF)
    pre = ein("erd,edh->erh", rows, w_up) + b_up_f[:, None, :]
    cdf, pdf = gelu_parts(pre)
    hid = (pre * cdf).astype(BF)
    res = (ein("erh,ehd->erd", hid, w_down) + b_down_f[:, None, :]).astype(BF)
    dpre = (ein("erd,ehd->erh", dres, w_down) * (cdf + pre * pdf)).astype(BF)
    din = ein("erh,edh->erd", dpre, w_up).astype(BF)
    dgate = jnp.sum(res.astype(F32) * dyr.astype(F32), axis=2)
    resg = (gate[:, :, None] * res.astype(F32)).astype(BF)
    part_b_up = jnp.sum(dpre.astype(F32), axis=1)
    part_b_down = jnp.sum(dres.astype(F32), axis=1)

    sends = []
    for s, g in enumerate(near_g):
        pickb = g[3]
        cut = lambda v: v[:, s * blocks * slots : (s + 1) * blocks * slots].reshape(
            local, blocks, slots, *v.shape[2:]
        )
        out_p = ein("bejt,ebjd->btd", pickb, cut(resg)).astype(BF)
        din_p = ein("bejt,ebjd->btd", pickb, cut(din)).astype(BF)
        dg = jnp.sum(pickb.astype(F32) * cut(dgate).transpose(1, 0, 2)[..., None], axis=2)
        dg_all = jnp.zeros((blocks, experts, ROWS), F32)
        dg_all = lax.dynamic_update_slice_in_dim(dg_all, dg, pl.ei * local, axis=1)
        sends.append((out_p, din_p, dg_all.astype(BF)))
    add = lambda a, b: (a.astype(F32) + b.astype(F32)).astype(a.dtype)
    pair = []
    for k in range(pl.nx):
        got = [pl.core(v) for v in sends[2 * k + 1]]
        pair.append([add(a, b) for a, b in zip(sends[2 * k], got)])
    total = pair[0]
    for k in range(1, pl.nx):
        got = [pl.xs(v, pl.nx - k) for v in pair[k]]
        total = [add(a, b) for a, b in zip(total, got)]
    moe = total[0][:, :SEQ].astype(F32)
    dchoice = total[1][:, :SEQ].astype(F32)
    dprob_all = total[2][:, :, :SEQ].astype(F32).transpose(0, 2, 1)
    block_out = (resid + moe).astype(BF).reshape(-1, width)

    rows2 = jnp.concatenate([rows, cat(far_g, 0)], axis=1)
    dyr2 = jnp.concatenate([dyr, cat(far_g, 1)], axis=1)
    gate2 = jnp.concatenate([gate, cat(far_g, 2)], axis=1)
    dres2 = (gate2[:, :, None] * dyr2.astype(F32)).astype(BF)
    ups, downs = [], []
    for kz in range(pl.nh):
        for ky in range(pl.ny):
            dest = (((pl.zh + kz) % pl.nh) * 2 + pl.zl) * pl.ny + (pl.y + ky) % pl.ny
            wu = lax.dynamic_slice_in_dim(w_up, dest * hb, hb, axis=2)
            wd = lax.dynamic_slice_in_dim(w_down, dest * hb, hb, axis=1)
            bu = lax.dynamic_slice_in_dim(b_up_f, dest * hb, hb, axis=1)
            pre = ein("erd,edh->erh", rows2, wu) + bu[:, None, :]
            cdf, pdf = gelu_parts(pre)
            hid = (pre * cdf).astype(BF)
            dpre = (ein("erd,ehd->erh", dres2, wd) * (cdf + pre * pdf)).astype(BF)
            downs.append(ein("erh,erd->ehd", hid, dres2).astype(BF))
            ups.append(ein("erd,erh->edh", rows2, dpre).astype(BF))

    def reduce_expert(vals):
        level = []
        for kz in range(pl.nh):
            mine = vals[kz * pl.ny].astype(F32)
            for ky in range(1, pl.ny):
                mine = mine + pl.ys(vals[kz * pl.ny + ky], ky).astype(F32)
            level.append(mine)
        mine = level[0]
        for kz in range(1, pl.nh):
            mine = mine + pl.zhs(level[kz].astype(BF), kz).astype(F32)
        return mine

    grad_up = reduce_expert(ups)
    grad_down = reduce_expert(downs)
    small = jnp.concatenate(
        [part_b_up.reshape(local, pl.nd, -1), part_b_down.reshape(local, pl.nd, -1)], axis=2
    ).transpose(1, 0, 2)
    small = small.reshape(pl.nz, pl.ny, local, -1)
    pick = lambda v, idx: lax.dynamic_index_in_dim(v, idx, 0, keepdims=False)
    small = pick(small, pl.z) + sum(
        pl.zs(pick(small, (pl.z + k) % pl.nz), k) for k in range(1, pl.nz)
    )
    small = pick(small, pl.y) + sum(
        pl.ys(pick(small, (pl.y + k) % pl.ny), k) for k in range(1, pl.ny)
    )
    grad_b_up, grad_b_down = small[:, :hb], small[:, hb:]

    dy_f = dy.astype(F32)
    dgates = [jnp.sum(o * dprob_all, axis=2, keepdims=True) for o in onehot]
    dprob = onehot[0] * dgates[0] + onehot[1] * dgates[1]
    dlogit = router * (dprob - jnp.sum(dprob * router, axis=-1, keepdims=True))
    dlogit = dlogit.astype(BF)
    g_router = ein("btd,bte->de", act_two, dlogit)
    dact_two = dchoice + ein("bte,de->btd", dlogit, full_router)
    dresid = dy_f + norm_back(dact_two, normed_two, inv_two, gain_two)
    dattn = dresid.astype(BF)
    g_proj = ein("btd,btf->df", mixed, dattn)
    dmixed = ein("btf,df->btd", dattn, full_proj).astype(BF).reshape(blocks, SEQ, heads, HEAD)
    probs_low = probs.astype(BF)
    dvalues = ein("ihst,ishd->ithd", probs_low, dmixed)
    dprobs = ein("ishd,ithd->ihst", dmixed, values)
    dscores = (probs * (dprobs - jnp.sum(dprobs * probs, axis=-1, keepdims=True))).astype(BF)
    dqueries = ein("ihst,ithd->ishd", dscores, keys) * score_scale
    dkeys = ein("ihst,ishd->ithd", dscores, queries) * score_scale
    dqkv = jnp.stack([dqueries, dkeys, dvalues], axis=2).reshape(blocks, SEQ, 3 * width).astype(BF)
    g_qkv = ein("btd,btf->df", act_one, dqkv)
    qkv_sums = jnp.sum(dqkv.astype(F32), axis=(0, 1))
    dact_one = ein("btf,df->btd", dqkv, full_qkv)
    grad_tokens = dresid + norm_back(dact_one, normed_one, inv_one, gain_one)
    g_vecs = jnp.stack(
        [
            jnp.sum(dact_one * normed_one, axis=(0, 1)),
            jnp.sum(dact_two * normed_two, axis=(0, 1)),
            qkv_sums[:width],
            qkv_sums[2 * width :],
            jnp.sum(dattn.astype(F32), axis=(0, 1)),
            jnp.sum(dact_one, axis=(0, 1)),
            jnp.sum(dact_two, axis=(0, 1)),
        ],
        axis=1,
    )
    grads = jnp.concatenate([g_qkv, g_proj, g_router, g_vecs], axis=1)
    grads = jnp.pad(grads, ((0, 0), (0, -cols % 128)))
    grads = scatter_rows(pl, grads)
    at = 4 * width
    return (
        block_out,
        grad_tokens.reshape(-1, width),
        grads[:, at + experts : at + experts + 2],
        grads[:, at + experts + 2 : at + experts + 7],
        grads[:, : 3 * width],
        grads[:, 3 * width : at],
        grads[:, at : at + experts],
        grad_up,
        grad_b_up,
        grad_down,
        grad_b_down,
    )


def solution(mesh):
    pl = Place(mesh)
    tok = P(("dp", "expert"), None)
    in_specs = (tok,) * 8 + (
        P("expert", None, None),
        P("expert", None),
        P("expert", None, None),
        P("expert", None),
    )
    out_specs = (tok,) * 7 + (
        P("expert", None, "dp"),
        P("expert", "dp"),
        P("expert", "dp", None),
        P("expert", "dp"),
    )

    def run(*args):
        return on_device(pl, *args)

    return jax.shard_map(run, mesh=mesh, in_specs=in_specs, out_specs=out_specs, check_vma=False)
```

```python
import functools

import jax
import jax.numpy as jnp
from jax import lax
from jax.experimental import pallas as pl
from jax.experimental.pallas import tpu as pltpu
from jax.sharding import PartitionSpec as P

HEAD = 64
SEQ = 197
MICRO = 4
HALF = 2
CORES = 2
EPSILON = 1e-06
BF = jnp.bfloat16
F32 = jnp.float32


LOW = -1e30


def cost(us):
    return pl.CostEstimate(flops=int(us * 0.35e9), bytes_accessed=1 << 20, transcendentals=0)


def dot(left, right, over_left, over_right):
    return lax.dot_general(
        left, right, (((over_left,), (over_right,)), ((), ())), preferred_element_type=F32
    )


def iota(shape, axis):
    return lax.broadcasted_iota(jnp.int32, shape, axis)


def norm_rows(row_block):
    row_mean = jnp.mean(row_block, axis=-1, keepdims=True)
    centred = row_block - row_mean
    inv_std = lax.rsqrt(jnp.mean(centred * centred, axis=-1, keepdims=True) + EPSILON)
    return (centred * inv_std, inv_std)


def norm_back(grad_h, normed, inv_std, gain_vec):
    scaled = grad_h * gain_vec
    return inv_std * (
        scaled
        - jnp.mean(scaled, axis=-1, keepdims=True)
        - normed * jnp.mean(scaled * normed, axis=-1, keepdims=True)
    )


def gelu_parts(pre_act):
    normal_cdf = 0.5 * (1.0 + lax.erf(pre_act * 0.7071067811865476))
    normal_pdf = jnp.exp(-0.5 * pre_act * pre_act) * 0.3989422804014327
    return (normal_cdf, normal_pdf)


def half_lanes(pair, side):
    lane = iota(pair.shape, 1)
    keep = lane < HEAD if side == 0 else lane >= HEAD
    return jnp.where(keep, pair, jnp.zeros_like(pair))


def router_rows(tailt, act, experts):
    logits = dot(tailt, act, 1, 1)[:experts]
    top = jnp.max(logits, axis=0, keepdims=True)
    powers = jnp.exp(logits - top)
    return powers / jnp.sum(powers, axis=0, keepdims=True)


def forward_kernel(experts, tok, dense, tailt, qkv_o, mix_o, res_o, act_o, lse_o):
    width = tok.shape[2]
    rows = tok.shape[1]
    pairs = width // (2 * HEAD)
    vec = tailt[...].astype(F32)[experts : experts + 7]
    x = tok[0].astype(F32)
    normed, _ = norm_rows(x)
    act = (normed * vec[0:1] + vec[5:6]).astype(BF)
    bias = jnp.concatenate([vec[2:3], jnp.zeros_like(vec[2:3]), vec[3:4]], axis=1)
    qkv_o[0] = (dot(act, dense[:, : 3 * width], 1, 0) + bias).astype(BF)
    seen = iota((rows, rows), 1) < SEQ
    lse_all = jnp.zeros((rows, 128), F32)
    lane = iota((rows, 128), 1)
    for p in range(pairs):
        at = p * 2 * HEAD
        q = qkv_o[0, :, at : at + 2 * HEAD]
        k = qkv_o[0, :, width + at : width + at + 2 * HEAD]
        v = qkv_o[0, :, 2 * width + at : 2 * width + at + 2 * HEAD]
        both = None
        for side in range(2):
            scores = dot(half_lanes(q, side), k, 1, 1) * (HEAD ** (-0.5))
            scores = jnp.where(seen, scores, LOW)
            top = jnp.max(scores, axis=1, keepdims=True)
            lse = top + jnp.log(jnp.sum(jnp.exp(scores - top), axis=1, keepdims=True))
            low = jnp.exp(scores - lse).astype(BF)
            part = dot(low, half_lanes(v, side), 1, 0)
            both = part if both is None else both + part
            lse_all = jnp.where(lane == 2 * p + side, lse, lse_all)
        mix_o[0, :, at : at + 2 * HEAD] = both.astype(BF)
    lse_o[0] = lse_all
    resid = x + (dot(mix_o[0], dense[:, 3 * width : 4 * width], 1, 0) + vec[4:5])
    res_o[0] = resid
    normed, _ = norm_rows(resid)
    act = (normed * vec[1:2] + vec[6:7]).astype(BF)
    act_o[0] = act
    gates = router_rows(tailt[...], act, experts)
    half = experts // 2
    blank = jnp.zeros((half, width // 2 - rows), F32)
    packed = jnp.concatenate([gates[:half], blank, gates[half:], blank], axis=1)
    act_o[0, rows - half :, :] = packed.astype(BF)


def run_forward(tok, dense, tailt, part, experts):
    _, rows, width = tok.shape
    whole = lambda a: pl.BlockSpec(a.shape, lambda i: (0,) * a.ndim)
    row = lambda n: pl.BlockSpec((1, rows, n), lambda i: (i, 0, 0))
    out = lambda n, d: jax.ShapeDtypeStruct((HALF, rows, n), d)
    return pl.pallas_call(
        functools.partial(forward_kernel, experts),
        grid=(HALF,),
        in_specs=[
            pl.BlockSpec((1, rows, width), lambda i: (part * HALF + i, 0, 0)),
            whole(dense),
            whole(tailt),
        ],
        out_specs=[row(3 * width), row(width), row(width), row(width), row(128)],
        out_shape=[out(3 * width, BF), out(width, BF), out(width, F32), out(width, BF), out(128, F32)],
        name="dense_forward",
        cost_estimate=cost(5),
        compiler_params=pltpu.CompilerParams(vmem_limit_bytes=60 << 20),
    )(tok, dense, tailt)


def packed_row(block, experts, e):
    rows, width = block.shape
    half = experts // 2
    table = block[rows - half :].astype(F32)
    side = e // half
    line = jnp.sum(jnp.where(iota(table.shape, 0) == e - side * half, table, 0.0), axis=0, keepdims=True)
    mid = width // 2
    return jnp.where(side == 0, line[:, :rows], line[:, mid : mid + rows])


def pick_rows(experts, local, slots, ei, sources, x_ref, g_ref, raw_ref, gate_ref, p_ref):
    for s, (act, dys) in enumerate(sources):
        for i in range(HALF):
            block = s * HALF + i
            at = block * slots
            rows, dyr = act[i], dys[i]
            hot, gates = [], []
            for j in range(local):
                slot = packed_row(dyr, experts, ei * local + j)
                gate = packed_row(rows, experts, ei * local + j)
                hit = iota((slots, rows.shape[0]), 0).astype(F32) == slot
                gates.append(jnp.sum(jnp.where(hit, gate, 0.0), axis=1, keepdims=True))
                hot.append(jnp.where(hit, 1.0, 0.0).astype(BF))
            hot = jnp.concatenate(hot, axis=0)
            x = dot(hot, rows, 1, 0).astype(BF)
            raw = dot(hot, dyr, 1, 0)
            if p_ref is not None:
                p_ref[block] = hot
            for j in range(local):
                cut = slice(j * slots, (j + 1) * slots)
                x_ref[j, at : at + slots, :] = x[cut]
                g_ref[j, at : at + slots, :] = (gates[j] * raw[cut]).astype(BF)
                if raw_ref is not None:
                    raw_ref[j, at : at + slots, :] = raw[cut].astype(BF)
                    gate_ref[j, at : at + slots, :] = jnp.broadcast_to(gates[j], (slots, 128))


def expert_kernel(experts, n_src, slots, chunk, ei_ref, *refs):
    acts, refs = refs[:n_src], refs[n_src:]
    dys, refs = refs[:n_src], refs[n_src:]
    wu, bu, wd, bd = refs[:4]
    out_near, out_far, x_ref, g_ref, gbu, gbd = refs[4:10]
    raw_ref, gate_ref, p_ref, resg_ref, din_ref, dg_ref = refs[10:]
    local = x_ref.shape[0]
    rows = acts[0].shape[1]
    hidden = wu.shape[2]
    ei = ei_ref[0]
    e = pl.program_id(0)

    @pl.when(e == 0)
    def _():
        pick_rows(
            experts, local, slots, ei, list(zip(acts, dys)), x_ref, g_ref, raw_ref, gate_ref, p_ref
        )

    x, g = x_ref[e], g_ref[e]
    res = din = None
    for h in range(0, hidden, chunk):
        cut = slice(h, h + chunk)
        up, down = wu[0, :, cut], wd[0, cut]
        pre = dot(x, up, 1, 0) + bu[0, :, cut].astype(F32)
        cdf, pdf = gelu_parts(pre)
        hid = (pre * cdf).astype(BF)
        dpre = (dot(g, down, 1, 1) * (cdf + pre * pdf)).astype(BF)
        gbu[0, :, cut] = jnp.sum(dpre.astype(F32), axis=0, keepdims=True)
        res_part, din_part = dot(hid, down, 1, 0), dot(dpre, up, 1, 1)
        res = res_part if res is None else res + res_part
        din = din_part if din is None else din + din_part
    gbd[0] = jnp.sum(g.astype(F32), axis=0, keepdims=True)
    res = (res + bd[0].astype(F32)).astype(BF).astype(F32)
    dg = jnp.sum(res * raw_ref[e].astype(F32), axis=1, keepdims=True)
    dg_ref[e] = jnp.broadcast_to(dg, dg_ref.shape[1:])
    resg_ref[e] = (gate_ref[e][:, 0:1] * res).astype(BF)
    din_ref[e] = din.astype(BF)

    @pl.when(e == local - 1)
    def _():
        for s in range(n_src):
            out = (out_near, out_far)[s % CORES]

            for i in range(HALF):
                block = s * HALF + i
                at = block * slots
                hot = p_ref[block]
                for kind, ref in enumerate((resg_ref, din_ref)):
                    part = jnp.concatenate([ref[j, at : at + slots, :] for j in range(local)], axis=0)
                    to = (kind * HALF + i) * rows
                    out[s // CORES, to : to + rows, :] = dot(hot, part, 0, 0).astype(BF)
                eid = iota((experts, rows), 0)
                dprob = jnp.zeros((experts, rows), F32)
                for j in range(local):
                    dg = dg_ref[j, at : at + slots, :][:, 0:1]
                    mine = hot[j * slots : (j + 1) * slots].astype(F32)
                    row = jnp.sum(mine * dg, axis=0, keepdims=True)
                    dprob = jnp.where(eid == ei * local + j, row, dprob)
                to = 2 * HALF * rows + i * experts
                out[s // CORES, to : to + experts, 0:rows] = dprob.astype(BF)


def run_experts(place, sources, w_up, b_up, w_down, b_down, experts, slots):
    local, width, hidden = w_up.shape
    n_src = len(sources)
    span = sources[0][0].shape[1]
    blocks = n_src * HALF
    rows = blocks * slots
    back = HALF * (2 * span + experts)
    flat = [s[i] for i in range(2) for s in sources]
    keep = lambda *s: pl.BlockSpec(s, lambda e, p: (0,) * len(s))
    each = lambda *s: pl.BlockSpec((1,) + s, lambda e, p: (e, 0, 0))
    return pl.pallas_call(
        functools.partial(expert_kernel, experts, n_src, slots, min(hidden, 1024)),
        grid_spec=pltpu.PrefetchScalarGridSpec(
            num_scalar_prefetch=1,
            grid=(local,),
            in_specs=[keep(HALF, span, width)] * len(flat)
            + [
                each(width, hidden),
                each(1, hidden),
                each(hidden, width),
                each(1, width),
            ],
            out_specs=[
                keep(n_src // CORES, back, width),
                keep(n_src // CORES, back, width),
                keep(local, rows, width),
                keep(local, rows, width),
                each(1, hidden),
                each(1, width),
            ],
            scratch_shapes=[
                pltpu.VMEM((local, rows, width), BF),
                pltpu.VMEM((local, rows, 128), F32),
                pltpu.VMEM((blocks, local * slots, span), BF),
                pltpu.VMEM((local, rows, width), BF),
                pltpu.VMEM((local, rows, width), BF),
                pltpu.VMEM((local, rows, 128), F32),
            ],
        ),
        out_shape=[
            jax.ShapeDtypeStruct((n_src // CORES, back, width), BF),
            jax.ShapeDtypeStruct((n_src // CORES, back, width), BF),
            jax.ShapeDtypeStruct((local, rows, width), BF),
            jax.ShapeDtypeStruct((local, rows, width), BF),
            jax.ShapeDtypeStruct((local, 1, hidden), F32),
            jax.ShapeDtypeStruct((local, 1, width), F32),
        ],
        name="experts",
        cost_estimate=cost(24),
        compiler_params=pltpu.CompilerParams(vmem_limit_bytes=60 << 20),
    )(place.ei.reshape(1), *flat, w_up, b_up, w_down, b_down)


def pick_kernel(experts, n_src, slots, ei_ref, *refs):
    x_ref, g_ref = refs[2 * n_src :]
    sources = list(zip(refs[:n_src], refs[n_src : 2 * n_src]))
    pick_rows(experts, x_ref.shape[0], slots, ei_ref[0], sources, x_ref, g_ref, None, None, None)


def run_pick(place, part, sources, local, experts, slots):
    _, span, width = sources[0][0].shape
    n_src = len(sources)
    rows = n_src * HALF * slots
    flat = [s[i] for i in range(2) for s in sources]
    half = lambda h: pl.BlockSpec((HALF, span, width), lambda i, p: (h, 0, 0))
    keep = pl.BlockSpec((local, rows, width), lambda i, p: (0, 0, 0))
    return pl.pallas_call(
        functools.partial(pick_kernel, experts, n_src, slots),
        grid_spec=pltpu.PrefetchScalarGridSpec(
            num_scalar_prefetch=1,
            grid=(1,),
            in_specs=[half(0)] * n_src + [half(part)] * n_src,
            out_specs=[keep] * 2,
        ),
        out_shape=[jax.ShapeDtypeStruct((local, rows, width), BF)] * 2,
        name="pick_rows",
        cost_estimate=cost(5),
        compiler_params=pltpu.CompilerParams(vmem_limit_bytes=60 << 20),
    )(place.ei.reshape(1), *flat)


def weight_grad_kernel(n_rows, ny, hb, own_ref, *refs):
    xs, gs = refs[:n_rows], refs[n_rows : 2 * n_rows]
    wu, bu, wd = refs[2 * n_rows : 2 * n_rows + 3]
    outs, total = refs[2 * n_rows + 3 : -1], refs[-1]
    up = down = None
    for x_ref, g_ref in zip(xs, gs):
        x, g = x_ref[0], g_ref[0]
        pre = dot(x, wu[0], 1, 0) + bu[0].astype(F32)
        cdf, pdf = gelu_parts(pre)
        hid = (pre * cdf).astype(BF)
        dpre = (dot(g, wd[0], 1, 1) * (cdf + pre * pdf)).astype(BF)
        down_part, up_part = dot(hid, g, 0, 0), dot(dpre, x, 0, 0)
        down = down_part if down is None else down + down_part
        up = up_part if up is None else up + up_part
    total[0] = up.astype(BF)
    total[1] = down.astype(BF)
    for k in range(ny):
        at = pl.multiple_of(lax.rem(own_ref[0] + k, ny) * hb, 16)
        outs[k][0] = total[:, pl.ds(at, hb), :]


def run_weight_grad(place, e, xs, gs, w_up, b_up, w_down):
    _, width, hidden = w_up.shape
    cols = hidden // place.nz
    nh, ny = place.nh, place.ny
    hb = cols // ny
    own = [place.y] + [(place.zh + k) % nh * 2 + place.zl for k in range(nh)]
    row = [pl.BlockSpec((1,) + x.shape[1:], lambda k, p: (e, 0, 0)) for x in xs]
    return pl.pallas_call(
        functools.partial(weight_grad_kernel, len(xs), ny, hb),
        grid_spec=pltpu.PrefetchScalarGridSpec(
            num_scalar_prefetch=1,
            grid=(nh,),
            in_specs=row
            + row
            + [
                pl.BlockSpec((1, width, cols), lambda k, p: (e, 0, p[k + 1])),
                pl.BlockSpec((1, 1, cols), lambda k, p: (e, 0, p[k + 1])),
                pl.BlockSpec((1, cols, width), lambda k, p: (e, p[k + 1], 0)),
            ],
            out_specs=[pl.BlockSpec((1, 2, hb, width), lambda k, p: (k, 0, 0, 0))] * ny,
            scratch_shapes=[pltpu.VMEM((2, cols, width), BF)],
        ),
        out_shape=[jax.ShapeDtypeStruct((nh, 2, hb, width), BF)] * ny,
        name="weight_grad",
        cost_estimate=cost(1),
        compiler_params=pltpu.CompilerParams(vmem_limit_bytes=60 << 20),
    )(jnp.stack(own).astype(jnp.int32), *xs, *gs, w_up, b_up, w_down)


def backward_kernel(experts, n_back, first, share, core_ref, *refs):
    tok, dy, dense, tailt, qkv, mix, resid, act_two, lse = refs[:9]
    moes, dins, dgs = [refs[9 + k * n_back : 9 + (k + 1) * n_back] for k in range(3)]
    refs = refs[9 + 3 * n_back :]
    if not first:
        before, before_t = refs[:2]
        refs = refs[2:]
    if share:
        out, gtok, keep, send, dqkv, acc, acc_t = refs
    else:
        out, gtok, acc, acc_t, dqkv = refs
    width = tok.shape[2]
    rows = tok.shape[1]
    pairs = width // (2 * HEAD)
    scale = HEAD ** (-0.5)

    @pl.when(pl.program_id(0) == 0)
    def _():
        if first:
            acc[...] = jnp.zeros_like(acc)
            acc_t[...] = jnp.zeros_like(acc_t)
        else:
            acc[:, : 4 * width] = before[...]
            acc_t[...] = before_t[...]

    total = lambda parts: functools.reduce(jnp.add, [p[...].astype(F32) for p in parts])
    tail = tailt[...]
    vec = tail.astype(F32)[experts : experts + 7]
    res = resid[0]
    out[0] = (res + total(moes)).astype(BF)
    normed_two, inv_two = norm_rows(res)
    probs = router_rows(tail, act_two[0], experts)
    dprob = total(dgs)[:, 0:rows]
    dlogit = probs * (dprob - jnp.sum(dprob * probs, axis=0, keepdims=True))
    dlogit = jnp.concatenate([dlogit, jnp.zeros((128 - experts, rows), F32)], axis=0).astype(BF)
    dact_two = total(dins) + dot(dlogit, tail, 0, 0)
    dyf = jnp.where(iota((rows, width), 0) < SEQ, dy[0].astype(F32), 0.0)
    dresid = dyf + norm_back(dact_two, normed_two, inv_two, vec[1:2])
    dattn = dresid.astype(BF)
    acc[:, 3 * width : 4 * width] += dot(mix[0], dattn, 0, 0)
    dmixed = dot(dattn, dense[:, 3 * width : 4 * width], 1, 1).astype(BF)
    seen = iota((rows, rows), 1) < SEQ
    for p in range(pairs):
        at = p * 2 * HEAD
        q = qkv[0, :, at : at + 2 * HEAD]
        k = qkv[0, :, width + at : width + at + 2 * HEAD]
        v = qkv[0, :, 2 * width + at : 2 * width + at + 2 * HEAD]
        dm = dmixed[:, at : at + 2 * HEAD]
        dq = dk = dv = None
        for side in range(2):
            q_s, dm_s = half_lanes(q, side), half_lanes(dm, side)
            scores = dot(q_s, k, 1, 1) * scale
            which = 2 * p + side
            weights = jnp.exp(jnp.where(seen, scores, LOW) - lse[0][:, which : which + 1])
            low = weights.astype(BF)
            dv_s = dot(low, dm_s, 0, 0)
            dw = dot(dm_s, v, 1, 1)
            ds = (weights * (dw - jnp.sum(dw * weights, axis=1, keepdims=True))).astype(BF)
            dq_s = dot(ds, half_lanes(k, side), 1, 0)
            dk_s = dot(ds, q_s, 0, 0)
            dq = dq_s if dq is None else dq + dq_s
            dk = dk_s if dk is None else dk + dk_s
            dv = dv_s if dv is None else dv + dv_s
        dqkv[:, at : at + 2 * HEAD] = (dq * scale).astype(BF)
        dqkv[:, width + at : width + at + 2 * HEAD] = (dk * scale).astype(BF)
        dqkv[:, 2 * width + at : 2 * width + at + 2 * HEAD] = dv.astype(BF)
    normed_one, inv_one = norm_rows(tok[0].astype(F32))
    act_one = (normed_one * vec[0:1] + vec[5:6]).astype(BF)
    acc[:, : 3 * width] += dot(act_one, dqkv[...], 0, 0)
    dact_one = dot(dqkv[...], dense[:, : 3 * width], 1, 1)
    gtok[0] = dresid + norm_back(dact_one, normed_one, inv_one, vec[0:1])
    rowsum = lambda v: jnp.sum(v.astype(F32), axis=0, keepdims=True)
    sums = [
        rowsum(dact_one * normed_one),
        rowsum(dact_two * normed_two),
        rowsum(dqkv[:, :width]),
        rowsum(dqkv[:, 2 * width :]),
        rowsum(dattn),
        rowsum(dact_one),
        rowsum(dact_two),
    ]
    acc_t[...] += dot(dlogit, act_two[0], 1, 0)
    for i, row in enumerate(sums):
        acc_t[experts + i : experts + i + 1, :] += row
    if share:

        @pl.when(pl.program_id(0) == HALF - 1)
        def _():
            last = jnp.transpose(acc_t[...], (1, 0))
            acc[:, 4 * width : 4 * width + 128] = last
            core = core_ref[0]

            def body(i, carry):
                to = pl.multiple_of(i * share, 16)
                for ref, side in ((keep, core), (send, 1 - core)):
                    at = pl.multiple_of((i * CORES + side) * share, 16)
                    ref[pl.ds(to, share), :] = acc[pl.ds(at, share), :].astype(BF)
                return carry

            lax.fori_loop(0, width // share // CORES, body, 0)


def run_backward(place, part, tok, dy, dense, tailt, saved, backs, before, experts, share):
    _, rows, width = tok.shape
    whole = lambda a: pl.BlockSpec(a.shape, lambda i, c: (0,) * len(a.shape))
    at_half = pl.BlockSpec((1, rows, width), lambda i, c: (part * HALF + i, 0, 0))
    row = lambda n: pl.BlockSpec((1, rows, n), lambda i, c: (i, 0, 0))
    first = 2 * HALF * rows // experts
    back_specs = (
        [pl.BlockSpec((rows, width), lambda i, c: (i, 0))] * len(backs)
        + [pl.BlockSpec((rows, width), lambda i, c: (HALF + i, 0))] * len(backs)
        + [pl.BlockSpec((experts, width), lambda i, c: (first + i, 0))] * len(backs)
    )
    args = [tok, dy, dense, tailt, *saved, *backs, *backs, *backs]
    specs = [at_half, at_half, whole(dense), whole(tailt)]
    specs += [row(3 * width), row(width), row(width), row(width), row(128)] + back_specs
    cols = dense.shape[1]
    scratch = [pltpu.VMEM((rows, 3 * width), BF)]
    if share:
        sums = [jax.ShapeDtypeStruct((width // CORES, cols), BF)] * 2
        scratch += [pltpu.VMEM((width, cols), F32), pltpu.VMEM((128, width), F32)]
    else:
        sums = [
            jax.ShapeDtypeStruct((width, 4 * width), F32),
            jax.ShapeDtypeStruct((128, width), F32),
        ]
    if before is not None:
        args += list(before)
        specs += [whole(b) for b in before]
    return pl.pallas_call(
        functools.partial(backward_kernel, experts, len(backs), before is None, share),
        grid_spec=pltpu.PrefetchScalarGridSpec(
            num_scalar_prefetch=1,
            grid=(HALF,),
            in_specs=specs,
            out_specs=[row(width), row(width), whole(sums[0]), whole(sums[1])],
            scratch_shapes=scratch,
        ),
        out_shape=[
            jax.ShapeDtypeStruct((HALF, rows, width), BF),
            jax.ShapeDtypeStruct((HALF, rows, width), F32),
            *sums,
        ],
        name="dense_backward",
        cost_estimate=cost(1),
        compiler_params=pltpu.CompilerParams(vmem_limit_bytes=60 << 20),
    )(place.c.reshape(1), *args)


def arrange_kernel(n, share, at_ref, near, other, dense, tailt):
    def body(i, carry):
        at = pl.multiple_of(i * share, 16)
        for k, ref in enumerate((near, other)):
            to = pl.multiple_of(at_ref[k * n + i] * share, 16)
            dense[pl.ds(to, share), :] = ref[pl.ds(at, share), :]
        return carry

    lax.fori_loop(0, n, body, 0)
    wide = dense.shape[1]
    tailt[...] = jnp.transpose(dense[:, wide - 128 :].astype(F32), (1, 0)).astype(BF)


def arrange(near, other, order, share):
    n = order.shape[0] // 2
    width, wide = 2 * near.shape[0], near.shape[1]
    vmem = pl.BlockSpec(memory_space=pltpu.VMEM)
    return pl.pallas_call(
        functools.partial(arrange_kernel, n, share),
        in_specs=[pl.BlockSpec(memory_space=pltpu.SMEM), vmem, vmem],
        out_specs=[vmem, vmem],
        out_shape=[
            jax.ShapeDtypeStruct((width, wide), BF),
            jax.ShapeDtypeStruct((128, width), BF),
        ],
        name="arrange",
        compiler_params=pltpu.CompilerParams(vmem_limit_bytes=60 << 20),
        cost_estimate=cost(3),
    )(order, near, other)


class Place:
    def __init__(self, mesh):
        self.ne = mesh.shape["expert"]
        self.nd = mesh.shape["dp"]
        self.nx = self.ne // CORES
        bits = self.nd.bit_length() - 1
        self.ny = 1 << (bits // 2)
        self.nz = self.nd // self.ny
        self.nh = self.nz // 2

    def here(self):
        ei = lax.axis_index("expert")
        di = lax.axis_index("dp")
        self.ei, self.di = ei, di
        self.x, self.c = ei // CORES, ei % CORES
        self.z, self.y = di // self.ny, di % self.ny
        self.zh, self.zl = self.z // 2, self.z % 2

    def core(self, val):
        return lax.ppermute(val, "expert", [(i, i ^ 1) for i in range(self.ne)])

    def xs(self, val, k):
        n, c = self.nx, CORES
        return lax.ppermute(val, "expert", [(i, (i // c + k) % n * c + i % c) for i in range(self.ne)])

    def ys(self, val, k):
        n = self.ny
        return lax.ppermute(val, "dp", [(i, i // n * n + (i + k) % n) for i in range(self.nd)])

    def zs(self, val, k):
        n, m = self.nz, self.ny
        return lax.ppermute(val, "dp", [(i, (i // m + k) % n * m + i % m) for i in range(self.nd)])

    def zp(self, val):
        n, m = self.nz, self.ny
        return lax.ppermute(val, "dp", [(i, (i // m ^ 1) * m + i % m) for i in range(self.nd)])

    def zhs(self, val, k):
        n, m = self.nh, self.ny
        return lax.ppermute(
            val,
            "dp",
            [(i, ((i // m // 2 + k) % n * 2 + i // m % 2) * m + i % m) for i in range(self.nd)],
        )

    def xy(self, val, kx, ky):
        def move(i):
            d, e = i // self.ne, i % self.ne
            d = d // self.ny * self.ny + (d + ky) % self.ny
            e = (e // CORES + kx) % self.nx * CORES + e % CORES
            return d * self.ne + e

        return lax.ppermute(val, ("dp", "expert"), [(i, move(i)) for i in range(self.nd * self.ne)])

    def group(self, val):
        mine = [val] + [self.xs(val, k) for k in range(1, self.nx)]
        other = [self.core(v) for v in mine]
        return [v for pair in zip(mine, other) for v in pair]


def after(val, *deps):
    return lax.optimization_barrier((val, *deps))[0]


def gather_dense(place, piece):
    share, wide = piece.shape
    nz, ny, nx = place.nz, place.ny, place.nx
    line = jnp.concatenate([piece] + [place.zs(piece, k) for k in range(1, nz)], axis=0)
    moves = [(ky, kx) for ky in range(ny) for kx in range(nx)]
    near = jnp.concatenate([line] + [place.xy(line, kx, ky) for ky, kx in moves[1:]], axis=0)
    other = place.core(near)
    order = []
    for c in (place.c, 1 - place.c):
        for ky, kx in moves:
            for kz in range(nz):
                dp = (place.z - kz) % nz * ny + (place.y - ky) % ny
                order.append(dp * place.ne + (place.x - kx) % nx * CORES + c)
    order = jnp.stack(order).astype(jnp.int32)
    if share % 16 == 0:
        return line, near, *arrange(near, other, order, share)
    full = jnp.concatenate([near, other]).reshape(-1, share, wide)
    dense = jnp.zeros_like(full).at[order].set(full).reshape(-1, wide)
    return line, near, dense, dense[:, wide - 128 :].T


def scatter_rows(place, keep, send, small, used, first, second, third):
    wide = keep.shape[1]
    add = lambda a, b: (a.astype(F32) + b.astype(F32)).astype(BF)

    def stage(v, n, own, shift, last=False):
        pick = lambda i: lax.dynamic_index_in_dim(v, i % n, 0, keepdims=False)
        total = pick(own).astype(F32)
        for k in range(1, n):
            total = total + shift(pick(own + k), k).astype(F32)
        return total if last else total.astype(BF)

    val = after(add(keep, place.core(after(send, *first))), *second)
    val = val.reshape(place.nz, place.ny, place.nx, -1, wide)
    val = stage(jnp.moveaxis(val, 2, 0), place.nx, place.x, place.xs)
    val = after(val, *third)
    val = jnp.concatenate([val[..., :used], small, val[..., used + small.shape[-1] :]], axis=-1)
    val = stage(jnp.moveaxis(val, 1, 0), place.ny, place.y, place.ys)
    return stage(val, place.nz, place.z, place.zs, last=True)


def on_device(
    place,
    tokens_in,
    grad_out,
    routes,
    norm_gains,
    biases,
    w_qkv,
    w_proj,
    w_router,
    w_up,
    b_up,
    w_down,
    b_down,
):
    place.here()
    width = tokens_in.shape[1]
    local, _, hidden = w_up.shape
    experts = local * place.ne
    cap = max(2, (2 * SEQ * 13 + 8 * experts - 1) // (8 * experts))
    slots = -(-cap // 16) * 16
    rows = -(-(SEQ + experts // 2) // 16) * 16
    hb = hidden // place.nd
    nh, ny = place.nh, place.ny
    share = w_qkv.shape[0]
    halves = range(MICRO // HALF)

    n_small = -(-local * (hb + width // place.nd) // share)
    used = experts + 7
    assert used + n_small <= 128 or share % 16
    piece = jnp.concatenate([w_qkv, w_proj, w_router, norm_gains, biases], axis=1)
    piece = jnp.pad(piece, ((0, 0), (0, 4 * width + 128 - piece.shape[1])))
    line, near, dense, tailt = gather_dense(place, piece)

    route_rows = routes.reshape(MICRO, SEQ, 2)
    names = jnp.arange(experts, dtype=jnp.int32)
    sel = jnp.any(route_rows[:, :, :, None] == names, axis=2)
    tri = (jnp.arange(SEQ)[:, None] >= jnp.arange(SEQ)[None, :]).astype(BF)
    pos = jnp.einsum("ts,bse->bet", tri, sel.astype(BF), preferred_element_type=F32)
    pos = jnp.where(sel.transpose(0, 2, 1), pos - 1, -1).astype(BF)
    pos = jnp.pad(pos, ((0, 0), (0, 0), (0, width // 2 - SEQ)), constant_values=-1)
    pos = jnp.concatenate([pos[:, : experts // 2], pos[:, experts // 2 :]], axis=2)

    blocks = lambda v: v.reshape(MICRO, SEQ, width)
    tok = jnp.pad(blocks(tokens_in), ((0, 0), (0, rows - SEQ), (0, 0)))
    gap = jnp.zeros((MICRO, rows - SEQ - experts // 2, width), BF)
    dy = jnp.concatenate([blocks(grad_out), gap, pos], axis=1)
    bu3, bd3 = b_up[:, None, :], b_down[:, None, :]
    dys = [dy[h * HALF : (h + 1) * HALF] for h in halves]
    dy_near = [place.group(dys[0])] + [place.group(after(d, near)) for d in dys[1:]]
    dy_z = place.zp(after(dy, line))

    saved, acts = [], []
    for h in halves:
        *keep, act, lse = run_forward(tok, dense, tailt, h, experts)
        saved.append((*keep, act, lse))
        acts.append(act)
    crossed = [[place.xs(act, k) for k in range(1, place.nx)] for act in acts]
    near, far = [], []
    for h in halves:
        mine = [acts[h], *crossed[h]]
        other = [place.core(after(v, acts[-1])) for v in mine]
        near.append([v for pair in zip(mine, other) for v in pair])
    for h in halves:
        far.append(place.group(after(place.zp(acts[h]), *crossed[-1])))
    dy_far = place.group(after(dy_z, *crossed[-1]))
    results, x_far, g_far = [], [], []
    for h in halves:
        src = list(zip(near[h], dy_near[h]))
        for at in range(0, len(src), 4):
            results.append(
                run_experts(place, src[at : at + 4], w_up, bu3, w_down, bd3, experts, slots)
            )
    for h in halves:
        src = list(zip(far[h], dy_far))
        for at in range(0, len(src), 4):
            x, g = run_pick(place, h, src[at : at + 4], local, experts, slots)
            x_far.append(x)
            g_far.append(g)

    xs = [r[2] for r in results] + x_far
    gs = [r[3] for r in results] + g_far
    add = lambda a, b: (a.astype(F32) + b.astype(F32)).astype(BF)

    def to_y(vals, *deps):
        mine = after(vals[0], *deps) if deps else vals[0]
        for ky in range(1, ny):
            mine = add(mine, place.ys(vals[ky], ky))
        return mine

    def to_z(mine):
        out = mine[0].astype(F32)
        for kz in range(1, nh):
            out = out + place.zhs(mine[kz], kz).astype(F32)
        return out

    part_b_up = sum(r[4] for r in results).reshape(local, place.nd, -1)
    part_b_down = sum(r[5] for r in results).reshape(local, place.nd, -1)
    small = jnp.concatenate([part_b_up, part_b_down], axis=2).transpose(1, 0, 2)
    small = small.reshape(place.nd, -1)
    small = jnp.pad(small, ((0, 0), (0, share * n_small - small.shape[1])))
    small = small.reshape(place.nz, ny, share, n_small).astype(BF)

    backs = []
    per = len(results) // len(halves)
    for h in halves:
        pair = [add(r[0], place.core(r[1])) for r in results[h * per : (h + 1) * per]]
        pair = [p[k] for p in pair for k in range(p.shape[0])]
        backs.append([pair[0]] + [place.xs(pair[k], place.nx - k) for k in range(1, place.nx)])

    sums = None
    outs, gtoks, sent, summed = [], [], [], []

    def weights(e, *deps):
        if e >= local:
            return
        first = after(xs[0], *deps) if deps else xs[0]
        sent.append(run_weight_grad(place, e, [first, *xs[1:]], gs, w_up, bu3, w_down))

    def tokens_back(h, *deps):
        nonlocal sums
        last = share if h == len(halves) - 1 and share % 16 == 0 else 0
        grads = after(dy, *deps)
        out, gtok, *sums = run_backward(
            place, h, tok, grads, dense, tailt, saved[h], backs[h], sums, experts, last
        )
        outs.append(out)
        gtoks.append(gtok)

    weights(0)
    weights(1, sent[0][0])
    tokens_back(0, sent[1][0])
    summed.append(to_y(sent[0], gtoks[0]))
    weights(2, gtoks[0], summed[0])
    weights(3, sent[2][0])
    summed.append(to_y(sent[1], sent[3][0]))
    both = [to_z(summed[0])]
    tokens_back(1, sent[3][0], summed[1], both[0])
    summed.append(to_y(sent[2], gtoks[1]))
    summed.append(to_y(sent[3], summed[2]))
    both += [to_z(v) for v in summed[1:]]
    grad_up = jnp.stack([b[0].T for b in both])
    grad_down = jnp.stack([b[1] for b in both])
    tokens = lambda v: jnp.concatenate(v, axis=0)[:, :SEQ].reshape(-1, width)
    if share % 16:
        full = jnp.concatenate([sums[0], sums[1].T], axis=1).astype(BF)
        full = jnp.moveaxis(full.reshape(-1, CORES, share, full.shape[1]), 1, 0)
        side = lambda c: lax.dynamic_index_in_dim(full, c, 0, keepdims=False)
        sums = [side(c).reshape(-1, full.shape[3]) for c in (place.c, 1 - place.c)]
    if used + n_small > 128:
        sums = [jnp.pad(v, ((0, 0), (0, used + n_small - 128))) for v in sums]
    waits = [summed[2]], [summed[3], both[1]], [both[2]]
    grads = scatter_rows(place, *sums, small, 4 * width + used, *waits)
    tiny = grads[:, 4 * width + used : 4 * width + used + n_small].reshape(-1)
    tiny = tiny[: local * (hb + width // place.nd)].reshape(local, -1)
    grad_b_up, grad_b_down = tiny[:, :hb], tiny[:, hb:]
    at = 4 * width
    return (
        tokens(outs),
        tokens(gtoks),
        grads[:, at + experts : at + experts + 2],
        grads[:, at + experts + 2 : at + experts + 7],
        grads[:, : 3 * width],
        grads[:, 3 * width : at],
        grads[:, at : at + experts],
        grad_up,
        grad_b_up,
        grad_down,
        grad_b_down,
    )


def solution(mesh):
    place = Place(mesh)
    tok = P(("dp", "expert"), None)
    in_specs = (tok,) * 8 + (
        P("expert", None, None),
        P("expert", None),
        P("expert", None, None),
        P("expert", None),
    )
    out_specs = (tok,) * 7 + (
        P("expert", None, "dp"),
        P("expert", "dp"),
        P("expert", "dp", None),
        P("expert", "dp"),
    )

    def run(*args):
        return on_device(place, *args)

    return jax.shard_map(run, mesh=mesh, in_specs=in_specs, out_specs=out_specs, check_vma=False)
```

```python
import functools

import jax
import jax.numpy as jnp
from jax import lax
from jax.experimental import pallas as pl
from jax.experimental.pallas import tpu as pltpu
from jax.sharding import PartitionSpec as P

HEAD = 64
SEQ = 197
MICRO = 4
HALF = 2
CORES = 2
EPSILON = 1e-06
BF = jnp.bfloat16
F32 = jnp.float32


LOW = -1e30


def cost(us):
    return pl.CostEstimate(flops=int(us * 0.35e9), bytes_accessed=1 << 20, transcendentals=0)


def dot(left, right, over_left, over_right):
    return lax.dot_general(
        left, right, (((over_left,), (over_right,)), ((), ())), preferred_element_type=F32
    )


def iota(shape, axis):
    return lax.broadcasted_iota(jnp.int32, shape, axis)


def norm_rows(row_block):
    row_mean = jnp.mean(row_block, axis=-1, keepdims=True)
    centred = row_block - row_mean
    inv_std = lax.rsqrt(jnp.mean(centred * centred, axis=-1, keepdims=True) + EPSILON)
    return (centred * inv_std, inv_std)


def norm_back(grad_h, normed, inv_std, gain_vec):
    scaled = grad_h * gain_vec
    return inv_std * (
        scaled
        - jnp.mean(scaled, axis=-1, keepdims=True)
        - normed * jnp.mean(scaled * normed, axis=-1, keepdims=True)
    )


def gelu_parts(pre_act):
    normal_cdf = 0.5 * (1.0 + lax.erf(pre_act * 0.7071067811865476))
    normal_pdf = jnp.exp(-0.5 * pre_act * pre_act) * 0.3989422804014327
    return (normal_cdf, normal_pdf)


def half_lanes(pair, side):
    lane = iota(pair.shape, 1)
    keep = lane < HEAD if side == 0 else lane >= HEAD
    return jnp.where(keep, pair, jnp.zeros_like(pair))


def router_rows(tailt, act, experts):
    logits = dot(tailt, act, 1, 1)[:experts]
    top = jnp.max(logits, axis=0, keepdims=True)
    powers = jnp.exp(logits - top)
    return powers / jnp.sum(powers, axis=0, keepdims=True)


def forward_kernel(experts, tok, dense, tailt, qkv_o, mix_o, res_o, act_o, lse_o):
    width = tok.shape[2]
    rows = tok.shape[1]
    pairs = width // (2 * HEAD)
    vec = tailt[...].astype(F32)[experts : experts + 7]
    x = tok[0].astype(F32)
    normed, _ = norm_rows(x)
    act = (normed * vec[0:1] + vec[5:6]).astype(BF)
    bias = jnp.concatenate([vec[2:3], jnp.zeros_like(vec[2:3]), vec[3:4]], axis=1)
    qkv_o[0] = (dot(act, dense[:, : 3 * width], 1, 0) + bias).astype(BF)
    seen = iota((rows, rows), 1) < SEQ
    lse_all = jnp.zeros((rows, 128), F32)
    lane = iota((rows, 128), 1)
    for p in range(pairs):
        at = p * 2 * HEAD
        q = qkv_o[0, :, at : at + 2 * HEAD]
        k = qkv_o[0, :, width + at : width + at + 2 * HEAD]
        v = qkv_o[0, :, 2 * width + at : 2 * width + at + 2 * HEAD]
        both = None
        for side in range(2):
            scores = dot(half_lanes(q, side), k, 1, 1) * (HEAD ** (-0.5))
            scores = jnp.where(seen, scores, LOW)
            top = jnp.max(scores, axis=1, keepdims=True)
            lse = top + jnp.log(jnp.sum(jnp.exp(scores - top), axis=1, keepdims=True))
            low = jnp.exp(scores - lse).astype(BF)
            part = dot(low, half_lanes(v, side), 1, 0)
            both = part if both is None else both + part
            lse_all = jnp.where(lane == 2 * p + side, lse, lse_all)
        mix_o[0, :, at : at + 2 * HEAD] = both.astype(BF)
    lse_o[0] = lse_all
    resid = x + (dot(mix_o[0], dense[:, 3 * width : 4 * width], 1, 0) + vec[4:5])
    res_o[0] = resid
    normed, _ = norm_rows(resid)
    act = (normed * vec[1:2] + vec[6:7]).astype(BF)
    act_o[0] = act
    gates = router_rows(tailt[...], act, experts)
    half = experts // 2
    blank = jnp.zeros((half, width // 2 - rows), F32)
    packed = jnp.concatenate([gates[:half], blank, gates[half:], blank], axis=1)
    act_o[0, rows - half :, :] = packed.astype(BF)


def run_forward(tok, dense, tailt, part, experts):
    _, rows, width = tok.shape
    whole = lambda a: pl.BlockSpec(a.shape, lambda i: (0,) * a.ndim)
    row = lambda n: pl.BlockSpec((1, rows, n), lambda i: (i, 0, 0))
    out = lambda n, d: jax.ShapeDtypeStruct((HALF, rows, n), d)
    return pl.pallas_call(
        functools.partial(forward_kernel, experts),
        grid=(HALF,),
        in_specs=[
            pl.BlockSpec((1, rows, width), lambda i: (part * HALF + i, 0, 0)),
            whole(dense),
            whole(tailt),
        ],
        out_specs=[row(3 * width), row(width), row(width), row(width), row(128)],
        out_shape=[out(3 * width, BF), out(width, BF), out(width, F32), out(width, BF), out(128, F32)],
        name="dense_forward",
        cost_estimate=cost(5),
        compiler_params=pltpu.CompilerParams(vmem_limit_bytes=24 << 20),
    )(tok, dense, tailt)


def packed_row(block, experts, e):
    rows, width = block.shape
    half = experts // 2
    table = block[rows - half :].astype(F32)
    side = e // half
    line = jnp.sum(jnp.where(iota(table.shape, 0) == e - side * half, table, 0.0), axis=0, keepdims=True)
    mid = width // 2
    return jnp.where(side == 0, line[:, :rows], line[:, mid : mid + rows])


def pick_rows(experts, local, slots, ei, sources, x_ref, g_ref, raw_ref, gate_ref, p_ref):
    for s, (act, dys) in enumerate(sources):
        for i in range(HALF):
            block = s * HALF + i
            at = block * slots
            rows, dyr = act[i], dys[i]
            hot, gates = [], []
            for j in range(local):
                slot = packed_row(dyr, experts, ei * local + j)
                gate = packed_row(rows, experts, ei * local + j)
                hit = iota((slots, rows.shape[0]), 0).astype(F32) == slot
                gates.append(jnp.sum(jnp.where(hit, gate, 0.0), axis=1, keepdims=True))
                hot.append(jnp.where(hit, 1.0, 0.0).astype(BF))
            hot = jnp.concatenate(hot, axis=0)
            x = dot(hot, rows, 1, 0).astype(BF)
            raw = dot(hot, dyr, 1, 0)
            if p_ref is not None:
                p_ref[block] = hot
            for j in range(local):
                cut = slice(j * slots, (j + 1) * slots)
                x_ref[j, at : at + slots, :] = x[cut]
                g_ref[j, at : at + slots, :] = (gates[j] * raw[cut]).astype(BF)
                if raw_ref is not None:
                    raw_ref[j, at : at + slots, :] = raw[cut].astype(BF)
                    gate_ref[j, at : at + slots, :] = jnp.broadcast_to(gates[j], (slots, 128))


def expert_kernel(experts, n_src, slots, chunk, at_ref, *refs):
    acts, refs = refs[:n_src], refs[n_src:]
    dys, refs = refs[:n_src], refs[n_src:]
    wu, bu, wd, bd = refs[:4]
    out_near, out_far, x_ref, g_ref, gbu, gbd = refs[4:10]
    raw_ref, gate_ref, p_ref, resg_ref, din_ref, dg_ref = refs[10:]
    local = x_ref.shape[0]
    rows = acts[0].shape[1]
    ei = at_ref[0]
    e = pl.program_id(0)

    @pl.when(e == 0)
    def _():
        pick_rows(
            experts, local, slots, ei, list(zip(acts, dys)), x_ref, g_ref, raw_ref, gate_ref, p_ref
        )

    x, g = x_ref[e], g_ref[e]
    res = din = None
    for h in range(0, wu.shape[2], chunk):
        cut = slice(h, h + chunk)
        up, down = wu[0, :, cut], wd[0, cut]
        pre = dot(x, up, 1, 0) + bu[pl.ds(e, 1), cut]
        cdf, pdf = gelu_parts(pre)
        hid = (pre * cdf).astype(BF)
        dpre = (dot(g, down, 1, 1) * (cdf + pre * pdf)).astype(BF)
        gbu[0, :, cut] = jnp.sum(dpre.astype(F32), axis=0, keepdims=True)
        res_part, din_part = dot(hid, down, 1, 0), dot(dpre, up, 1, 1)
        res = res_part if res is None else res + res_part
        din = din_part if din is None else din + din_part
    gbd[0] = jnp.sum(g.astype(F32), axis=0, keepdims=True)
    res = (res + bd[pl.ds(e, 1), :]).astype(BF).astype(F32)
    dg = jnp.sum(res * raw_ref[e].astype(F32), axis=1, keepdims=True)
    dg_ref[e] = jnp.broadcast_to(dg, dg_ref.shape[1:])
    resg_ref[e] = (gate_ref[e][:, 0:1] * res).astype(BF)
    din_ref[e] = din.astype(BF)

    @pl.when(e == local - 1)
    def _():
        for s in range(n_src):
            out = (out_near, out_far)[s % CORES]

            for i in range(HALF):
                block = s * HALF + i
                at = block * slots
                hot = p_ref[block]
                for kind, ref in enumerate((resg_ref, din_ref)):
                    part = jnp.concatenate([ref[j, at : at + slots, :] for j in range(local)], axis=0)
                    to = (kind * HALF + i) * rows
                    out[s // CORES, to : to + rows, :] = dot(hot, part, 0, 0).astype(BF)
                eid = iota((experts, rows), 0)
                dprob = jnp.zeros((experts, rows), F32)
                for j in range(local):
                    dg = dg_ref[j, at : at + slots, :][:, 0:1]
                    mine = hot[j * slots : (j + 1) * slots].astype(F32)
                    row = jnp.sum(mine * dg, axis=0, keepdims=True)
                    dprob = jnp.where(eid == ei * local + j, row, dprob)
                to = 2 * HALF * rows + i * experts
                out[s // CORES, to : to + experts, 0:rows] = dprob.astype(BF)


def run_experts(place, part, sources, w_up, b_up, w_down, b_down, experts, slots):
    local, width, hidden = w_up.shape
    n_src = len(sources)
    span = sources[0][0].shape[1]
    blocks = n_src * HALF
    rows = blocks * slots
    back = HALF * (2 * span + experts)
    flat = [s[i] for i in range(2) for s in sources]
    keep = lambda *s: pl.BlockSpec(s, lambda e, p: (0,) * len(s))
    each = lambda *s: pl.BlockSpec((1,) + s, lambda e, p: (e, 0, 0))
    return pl.pallas_call(
        functools.partial(expert_kernel, experts, n_src, slots, min(hidden, 1024)),
        grid_spec=pltpu.PrefetchScalarGridSpec(
            num_scalar_prefetch=1,
            grid=(local,),
            in_specs=[keep(HALF, span, width)] * n_src
            + [pl.BlockSpec((HALF, span, width), lambda e, p: (part, 0, 0))] * n_src
            + [
                each(width, hidden),
                keep(local, hidden),
                each(hidden, width),
                keep(local, width),
            ],
            out_specs=[
                keep(n_src // CORES, back, width),
                keep(n_src // CORES, back, width),
                keep(local, rows, width),
                keep(local, rows, width),
                each(1, hidden),
                each(1, width),
            ],
            scratch_shapes=[
                pltpu.VMEM((local, rows, width), BF),
                pltpu.VMEM((local, rows, 128), F32),
                pltpu.VMEM((blocks, local * slots, span), BF),
                pltpu.VMEM((local, rows, width), BF),
                pltpu.VMEM((local, rows, width), BF),
                pltpu.VMEM((local, rows, 128), F32),
            ],
        ),
        out_shape=[
            jax.ShapeDtypeStruct((n_src // CORES, back, width), BF),
            jax.ShapeDtypeStruct((n_src // CORES, back, width), BF),
            jax.ShapeDtypeStruct((local, rows, width), BF),
            jax.ShapeDtypeStruct((local, rows, width), BF),
            jax.ShapeDtypeStruct((local, 1, hidden), F32),
            jax.ShapeDtypeStruct((local, 1, width), F32),
        ],
        name="experts",
        cost_estimate=cost(24),
        compiler_params=pltpu.CompilerParams(vmem_limit_bytes=60 << 20),
    )(place.ei.reshape(1), *flat, w_up, b_up, w_down, b_down)


def pick_kernel(experts, n_src, slots, ei_ref, *refs):
    x_ref, g_ref = refs[2 * n_src :]
    sources = list(zip(refs[:n_src], refs[n_src : 2 * n_src]))
    pick_rows(experts, x_ref.shape[0], slots, ei_ref[0], sources, x_ref, g_ref, None, None, None)


def run_pick(place, part, sources, local, experts, slots):
    _, span, width = sources[0][0].shape
    n_src = len(sources)
    rows = n_src * HALF * slots
    flat = [s[i] for i in range(2) for s in sources]
    half = lambda h: pl.BlockSpec((HALF, span, width), lambda i, p: (h, 0, 0))
    keep = pl.BlockSpec((local, rows, width), lambda i, p: (0, 0, 0))
    return pl.pallas_call(
        functools.partial(pick_kernel, experts, n_src, slots),
        grid_spec=pltpu.PrefetchScalarGridSpec(
            num_scalar_prefetch=1,
            grid=(1,),
            in_specs=[half(0)] * n_src + [half(part)] * n_src,
            out_specs=[keep] * 2,
        ),
        out_shape=[jax.ShapeDtypeStruct((local, rows, width), BF)] * 2,
        name="pick_rows",
        cost_estimate=cost(1),
        compiler_params=pltpu.CompilerParams(vmem_limit_bytes=32 << 20),
    )(place.ei.reshape(1), *flat)


def weight_grad_kernel(e, n_rows, ny, hb, own_ref, *refs):
    xs, gs = refs[:n_rows], refs[n_rows : 2 * n_rows]
    wu, bu, wd = refs[2 * n_rows : 2 * n_rows + 3]
    outs, total = refs[2 * n_rows + 3 : -1], refs[-1]
    up = down = None
    for x_ref, g_ref in zip(xs, gs):
        x, g = x_ref[0], g_ref[0]
        pre = dot(x, wu[0], 1, 0) + bu[e : e + 1, :]
        cdf, pdf = gelu_parts(pre)
        hid = (pre * cdf).astype(BF)
        dpre = (dot(g, wd[0], 1, 1) * (cdf + pre * pdf)).astype(BF)
        down_part, up_part = dot(hid, g, 0, 0), dot(dpre, x, 0, 0)
        down = down_part if down is None else down + down_part
        up = up_part if up is None else up + up_part
    total[0] = up.astype(BF)
    total[1] = down.astype(BF)
    for k in range(ny):
        at = pl.multiple_of(lax.rem(own_ref[0] + k, ny) * hb, 16)
        outs[k][0] = total[:, pl.ds(at, hb), :]


def run_weight_grad(place, where, e, xs, gs, w_up, b_up, w_down):
    _, width, hidden = w_up.shape
    cols = hidden // place.nz
    nh, ny = place.nh, place.ny
    hb = cols // ny
    row = [pl.BlockSpec((1,) + x.shape[1:], lambda k, p: (e, 0, 0)) for x in xs]
    return pl.pallas_call(
        functools.partial(weight_grad_kernel, e, len(xs), ny, hb),
        grid_spec=pltpu.PrefetchScalarGridSpec(
            num_scalar_prefetch=1,
            grid=(nh,),
            in_specs=row
            + row
            + [
                pl.BlockSpec((1, width, cols), lambda k, p: (e, 0, p[k + 1])),
                pl.BlockSpec((b_up.shape[0], cols), lambda k, p: (0, p[k + 1])),
                pl.BlockSpec((1, cols, width), lambda k, p: (e, p[k + 1], 0)),
            ],
            out_specs=[pl.BlockSpec((1, 2, hb, width), lambda k, p: (k, 0, 0, 0))] * ny,
            scratch_shapes=[pltpu.VMEM((2, cols, width), BF)],
        ),
        out_shape=[jax.ShapeDtypeStruct((nh, 2, hb, width), BF)] * ny,
        name="weight_grad",
        cost_estimate=cost(1),
        compiler_params=pltpu.CompilerParams(vmem_limit_bytes=32 << 20),
    )(where, *xs, *gs, w_up, b_up, w_down)


def backward_kernel(experts, n_back, *refs):
    tok, dy, dense, tailt, qkv, resid, act_two, lse = refs[:8]
    moes, dins, dgs = [refs[8 + k * n_back : 8 + (k + 1) * n_back] for k in range(3)]
    out, gtok, dattn_o, act_o, dqkv, acc_t = refs[8 + 3 * n_back :]
    width = tok.shape[2]
    rows = tok.shape[1]
    pairs = width // (2 * HEAD)
    scale = HEAD ** (-0.5)
    total = lambda parts: functools.reduce(jnp.add, [p[...].astype(F32) for p in parts])
    tail = tailt[...]
    vec = tail.astype(F32)[experts : experts + 7]
    res = resid[0]
    out[0] = (res + total(moes)).astype(BF)
    normed_two, inv_two = norm_rows(res)
    probs = router_rows(tail, act_two[0], experts)
    dprob = total(dgs)[:, 0:rows]
    dlogit = probs * (dprob - jnp.sum(dprob * probs, axis=0, keepdims=True))
    dlogit = jnp.concatenate([dlogit, jnp.zeros((128 - experts, rows), F32)], axis=0).astype(BF)
    dact_two = total(dins) + dot(dlogit, tail, 0, 0)
    dyf = jnp.where(iota((rows, width), 0) < SEQ, dy[0].astype(F32), 0.0)
    dresid = dyf + norm_back(dact_two, normed_two, inv_two, vec[1:2])
    dattn = dresid.astype(BF)
    dattn_o[0] = dattn
    dmixed = dot(dattn, dense[:, 3 * width : 4 * width], 1, 1).astype(BF)
    seen = iota((rows, rows), 1) < SEQ
    for p in range(pairs):
        at = p * 2 * HEAD
        q = qkv[0, :, at : at + 2 * HEAD]
        k = qkv[0, :, width + at : width + at + 2 * HEAD]
        v = qkv[0, :, 2 * width + at : 2 * width + at + 2 * HEAD]
        dm = dmixed[:, at : at + 2 * HEAD]
        dq = dk = dv = None
        for side in range(2):
            q_s, dm_s = half_lanes(q, side), half_lanes(dm, side)
            scores = dot(q_s, k, 1, 1) * scale
            which = 2 * p + side
            weights = jnp.exp(jnp.where(seen, scores, LOW) - lse[0][:, which : which + 1])
            low = weights.astype(BF)
            dv_s = dot(low, dm_s, 0, 0)
            dw = dot(dm_s, v, 1, 1)
            ds = (weights * (dw - jnp.sum(dw * weights, axis=1, keepdims=True))).astype(BF)
            dq_s = dot(ds, half_lanes(k, side), 1, 0)
            dk_s = dot(ds, q_s, 0, 0)
            dq = dq_s if dq is None else dq + dq_s
            dk = dk_s if dk is None else dk + dk_s
            dv = dv_s if dv is None else dv + dv_s
        dqkv[0, :, at : at + 2 * HEAD] = (dq * scale).astype(BF)
        dqkv[0, :, width + at : width + at + 2 * HEAD] = (dk * scale).astype(BF)
        dqkv[0, :, 2 * width + at : 2 * width + at + 2 * HEAD] = dv.astype(BF)
    normed_one, inv_one = norm_rows(tok[0].astype(F32))
    act_one = (normed_one * vec[0:1] + vec[5:6]).astype(BF)
    act_o[0] = act_one
    dact_one = dot(dqkv[0], dense[:, : 3 * width], 1, 1)
    gtok[0] = dresid + norm_back(dact_one, normed_one, inv_one, vec[0:1])
    rowsum = lambda v: jnp.sum(v.astype(F32), axis=0, keepdims=True)
    sums = [
        rowsum(dact_one * normed_one),
        rowsum(dact_two * normed_two),
        rowsum(dqkv[0, :, :width]),
        rowsum(dqkv[0, :, 2 * width :]),
        rowsum(dattn),
        rowsum(dact_one),
        rowsum(dact_two),
    ]
    acc_t[...] = dot(dlogit, act_two[0], 1, 0)
    for i, row in enumerate(sums):
        acc_t[experts + i : experts + i + 1, :] = row


def run_backward(image, tok, dy, dense, tailt, saved, backs, experts):
    _, rows, width = tok.shape
    i = image % HALF
    whole = lambda a: pl.BlockSpec(a.shape, lambda k: (0,) * len(a.shape))
    at = lambda j, n: pl.BlockSpec((1, rows, n), lambda k: (j, 0, 0))
    first = 2 * HALF * rows // experts
    back_specs = (
        [pl.BlockSpec((rows, width), lambda k: (i, 0))] * len(backs)
        + [pl.BlockSpec((rows, width), lambda k: (HALF + i, 0))] * len(backs)
        + [pl.BlockSpec((experts, width), lambda k: (first + i, 0))] * len(backs)
    )
    qkv, _, resid, act, lse = saved
    args = [tok, dy, dense, tailt, qkv, resid, act, lse, *backs, *backs, *backs]
    specs = [at(image, width), at(image, width), whole(dense), whole(tailt)]
    specs += [at(i, 3 * width), at(i, width), at(i, width), at(i, 128)] + back_specs
    out = lambda n, d: jax.ShapeDtypeStruct((1, rows, n), d)
    outs = [out(width, BF), out(width, F32), out(width, BF), out(width, BF), out(3 * width, BF)]
    outs += [jax.ShapeDtypeStruct((128, width), F32)]
    return pl.pallas_call(
        functools.partial(backward_kernel, experts, len(backs)),
        grid=(1,),
        in_specs=specs,
        out_specs=[whole(o) for o in outs],
        out_shape=outs,
        name="dense_backward",
        cost_estimate=cost(1),
        compiler_params=pltpu.CompilerParams(vmem_limit_bytes=24 << 20),
    )(*args)


def dense_grads_kernel(share, core_ref, *refs):
    acts, dqkvs, dattns, tails = [refs[k * MICRO : (k + 1) * MICRO] for k in range(4)]
    mixes = refs[4 * MICRO : 4 * MICRO + MICRO // HALF]
    outs = refs[4 * MICRO + MICRO // HALF :]
    full = outs[-1]
    width = acts[0].shape[2]
    join = lambda parts: jnp.concatenate([p[0] for p in parts], axis=0)
    act, dqkv, dattn = join(acts), join(dqkvs), join(dattns)
    mix = jnp.concatenate([m[i] for m in mixes for i in range(HALF)], axis=0)
    for k in range(3):
        full[:, k * width : (k + 1) * width] = dot(
            act, dqkv[:, k * width : (k + 1) * width], 0, 0
        ).astype(BF)
    full[:, 3 * width : 4 * width] = dot(mix, dattn, 0, 0).astype(BF)
    tail = functools.reduce(jnp.add, [t[...] for t in tails])
    full[:, 4 * width :] = jnp.transpose(tail, (1, 0)).astype(BF)
    if share:
        keep, send = outs[:2]
        core = core_ref[0]

        def body(i, carry):
            to = pl.multiple_of(i * share, 16)
            for ref, side in ((keep, core), (send, 1 - core)):
                at = pl.multiple_of((i * CORES + side) * share, 16)
                ref[pl.ds(to, share), :] = full[pl.ds(at, share), :]
            return carry

        lax.fori_loop(0, width // share // CORES, body, 0)


def run_dense_grads(place, parts, mixes, wide, share):
    width = mixes[0].shape[2]
    args = [p[k] for k in (3, 4, 2, 5) for p in parts] + list(mixes)
    vmem = pl.BlockSpec(memory_space=pltpu.VMEM)
    whole = [jax.ShapeDtypeStruct((width, wide), BF)]
    split = [jax.ShapeDtypeStruct((width // CORES, wide), BF)] * 2
    return pl.pallas_call(
        functools.partial(dense_grads_kernel, share),
        in_specs=[pl.BlockSpec(memory_space=pltpu.SMEM)] + [vmem] * len(args),
        out_specs=[vmem] * len(split if share else whole),
        out_shape=split if share else whole,
        scratch_shapes=[pltpu.VMEM((width, wide), BF)] if share else [],
        name="dense_grads",
        cost_estimate=cost(1),
        compiler_params=pltpu.CompilerParams(vmem_limit_bytes=32 << 20),
    )(place.c.reshape(1), *args)


def store_expert_kernel(n, *refs):
    total = functools.reduce(jnp.add, [r[...].astype(F32) for r in refs[:n]])
    up, down = refs[-2:]
    up[0] = jnp.transpose(total[0], (1, 0))
    down[0] = total[1]


def store_expert(e, local, parts, before):
    _, hb, width = parts[0].shape
    whole = pl.BlockSpec(parts[0].shape, lambda k: (0, 0, 0))
    return pl.pallas_call(
        functools.partial(store_expert_kernel, len(parts)),
        grid=(1,),
        in_specs=[whole] * len(parts) + [pl.BlockSpec(memory_space=pl.ANY)] * len(before),
        out_specs=[
            pl.BlockSpec((1, width, hb), lambda k: (e, 0, 0)),
            pl.BlockSpec((1, hb, width), lambda k: (e, 0, 0)),
        ],
        out_shape=[
            jax.ShapeDtypeStruct((local, width, hb), F32),
            jax.ShapeDtypeStruct((local, hb, width), F32),
        ],
        input_output_aliases={len(parts) + k: k for k in range(len(before))},
        name="store_expert",
        cost_estimate=cost(1),
        compiler_params=pltpu.CompilerParams(vmem_limit_bytes=16 << 20),
    )(*parts, *before)


def split_kernel(n, *refs):
    total = functools.reduce(jnp.add, [r[...].astype(F32) for r in refs[:n]])
    at = 0
    for out in refs[n:]:
        out[...] = total[:, at : at + out.shape[1]]
        at += out.shape[1]


def split_sum(parts, widths):
    vmem = pl.BlockSpec(memory_space=pltpu.VMEM)
    return pl.pallas_call(
        functools.partial(split_kernel, len(parts)),
        in_specs=[vmem] * len(parts),
        out_specs=[vmem] * len(widths),
        out_shape=[jax.ShapeDtypeStruct((parts[0].shape[0], w), F32) for w in widths],
        name="split_sum",
        cost_estimate=cost(1),
        compiler_params=pltpu.CompilerParams(vmem_limit_bytes=16 << 20),
    )(*parts)


def arrange_kernel(n, share, at_ref, near, other, dense, tailt):
    def body(i, carry):
        at = pl.multiple_of(i * share, 16)
        for k, ref in enumerate((near, other)):
            to = pl.multiple_of(at_ref[k * n + i] * share, 16)
            dense[pl.ds(to, share), :] = ref[pl.ds(at, share), :]
        return carry

    lax.fori_loop(0, n, body, 0)
    wide = dense.shape[1]
    tailt[...] = jnp.transpose(dense[:, wide - 128 :].astype(F32), (1, 0)).astype(BF)


def arrange(near, other, order, share):
    n = order.shape[0] // 2
    width, wide = 2 * near.shape[0], near.shape[1]
    vmem = pl.BlockSpec(memory_space=pltpu.VMEM)
    return pl.pallas_call(
        functools.partial(arrange_kernel, n, share),
        in_specs=[pl.BlockSpec(memory_space=pltpu.SMEM), vmem, vmem],
        out_specs=[vmem, vmem],
        out_shape=[
            jax.ShapeDtypeStruct((width, wide), BF),
            jax.ShapeDtypeStruct((128, width), BF),
        ],
        name="arrange",
        compiler_params=pltpu.CompilerParams(vmem_limit_bytes=16 << 20),
        cost_estimate=cost(1),
    )(order, near, other)


class Place:
    def __init__(self, mesh):
        self.ne = mesh.shape["expert"]
        self.nd = mesh.shape["dp"]
        self.nx = self.ne // CORES
        bits = self.nd.bit_length() - 1
        self.ny = 1 << (bits // 2)
        self.nz = self.nd // self.ny
        self.nh = self.nz // 2

    def here(self):
        ei = lax.axis_index("expert")
        di = lax.axis_index("dp")
        self.ei, self.di = ei, di
        self.x, self.c = ei // CORES, ei % CORES
        self.z, self.y = di // self.ny, di % self.ny
        self.zh, self.zl = self.z // 2, self.z % 2

    def core(self, val):
        return lax.ppermute(val, "expert", [(i, i ^ 1) for i in range(self.ne)])

    def xs(self, val, k):
        n, c = self.nx, CORES
        return lax.ppermute(val, "expert", [(i, (i // c + k) % n * c + i % c) for i in range(self.ne)])

    def ys(self, val, k):
        n = self.ny
        return lax.ppermute(val, "dp", [(i, i // n * n + (i + k) % n) for i in range(self.nd)])

    def zs(self, val, k):
        n, m = self.nz, self.ny
        return lax.ppermute(val, "dp", [(i, (i // m + k) % n * m + i % m) for i in range(self.nd)])

    def zp(self, val):
        n, m = self.nz, self.ny
        return lax.ppermute(val, "dp", [(i, (i // m ^ 1) * m + i % m) for i in range(self.nd)])

    def zhs(self, val, k):
        n, m = self.nh, self.ny
        return lax.ppermute(
            val,
            "dp",
            [(i, ((i // m // 2 + k) % n * 2 + i // m % 2) * m + i % m) for i in range(self.nd)],
        )

    def xy(self, val, kx, ky):
        def move(i):
            d, e = i // self.ne, i % self.ne
            d = d // self.ny * self.ny + (d + ky) % self.ny
            e = (e // CORES + kx) % self.nx * CORES + e % CORES
            return d * self.ne + e

        return lax.ppermute(val, ("dp", "expert"), [(i, move(i)) for i in range(self.nd * self.ne)])

    def group(self, val):
        mine = [val] + [self.xs(val, k) for k in range(1, self.nx)]
        other = [self.core(v) for v in mine]
        return [v for pair in zip(mine, other) for v in pair]


def after(deps, *vals):
    return lax.optimization_barrier((*vals, *deps))[: len(vals)]


def place_order(place):
    nz, ny, nx = place.nz, place.ny, place.nx
    order = []
    for c in (place.c, 1 - place.c):
        for ky in range(ny):
            for kx in range(nx):
                for kz in range(nz):
                    dp = (place.z - kz) % nz * ny + (place.y - ky) % ny
                    order.append(dp * place.ne + (place.x - kx) % nx * CORES + c)
    return jnp.stack(order).astype(jnp.int32)


def dense_in_order(place, near, other, order, share):
    if share % 16 == 0:
        return arrange(near, other, order, share)
    wide = near.shape[1]
    full = jnp.concatenate([near, other]).reshape(-1, share, wide)
    dense = jnp.zeros_like(full).at[order].set(full).reshape(-1, wide)
    return dense, dense[:, wide - 128 :].T


def stage(v, n, own, shift, dtype=BF):
    pick = lambda i: lax.dynamic_index_in_dim(v, i % n, 0, keepdims=False)
    total = pick(own).astype(F32)
    for k in range(1, n):
        total = total + shift(pick(own + k), k).astype(F32)
    return total.astype(dtype)


def on_device(
    place,
    tokens_in,
    grad_out,
    routes,
    norm_gains,
    biases,
    w_qkv,
    w_proj,
    w_router,
    w_up,
    b_up,
    w_down,
    b_down,
):
    place.here()
    width = tokens_in.shape[1]
    local, _, hidden = w_up.shape
    experts = local * place.ne
    cap = max(2, (2 * SEQ * 13 + 8 * experts - 1) // (8 * experts))
    slots = -(-cap // 16) * 16
    rows = -(-(SEQ + experts // 2) // 16) * 16
    hb = hidden // place.nd
    nh, ny = place.nh, place.ny
    share = w_qkv.shape[0]
    halves = range(MICRO // HALF)

    n_small = -(-local * (hb + width // place.nd) // share)
    used = experts + 7
    assert used + n_small <= 128 or share % 16
    piece = jnp.concatenate([w_qkv, w_proj, w_router, norm_gains, biases], axis=1)
    piece = jnp.pad(piece, ((0, 0), (0, 4 * width + 128 - piece.shape[1])))

    route_rows = routes.reshape(MICRO, SEQ, 2)
    names = jnp.arange(experts, dtype=jnp.int32)
    sel = jnp.any(route_rows[:, :, :, None] == names, axis=2)
    tri = (jnp.arange(SEQ)[:, None] >= jnp.arange(SEQ)[None, :]).astype(BF)
    pos = jnp.einsum("ts,bse->bet", tri, sel.astype(BF), preferred_element_type=F32)
    pos = jnp.where(sel.transpose(0, 2, 1), pos - 1, -1).astype(BF)
    pos = jnp.pad(pos, ((0, 0), (0, 0), (0, width // 2 - SEQ)), constant_values=-1)
    pos = jnp.concatenate([pos[:, : experts // 2], pos[:, experts // 2 :]], axis=2)

    blocks = lambda v: v.reshape(MICRO, SEQ, width)
    tok = jnp.pad(blocks(tokens_in), ((0, 0), (0, rows - SEQ), (0, 0)))
    gap = jnp.zeros((MICRO, rows - SEQ - experts // 2, width), BF)
    dy = jnp.concatenate([blocks(grad_out), gap, pos], axis=1)
    bu3, bd3 = b_up.astype(F32), b_down.astype(F32)
    across = lambda v: [v] + [place.xs(v, k) for k in range(1, place.nx)]
    both_cores = lambda mine, other: [v for pair in zip(mine, other) for v in pair]
    both_cores = lambda mine, other: [v for pair in zip(mine, other) for v in pair]
    nx, nz = place.nx, place.nz

    line = [piece] + [place.zs(piece, k) for k in range(1, nz)]
    done = line

    (line,) = after(done, jnp.concatenate(line, axis=0))
    moves = [(ky, kx) for ky in range(ny) for kx in range(nx)]
    part = [line] + [place.xy(line, kx, ky) for ky, kx in moves[1:]]
    own = [(place.zh + k) % nh * 2 + place.zl for k in range(nh)]
    where = jnp.stack([place.y, *own]).astype(jnp.int32)
    tok, order, bu3, bd3, where = after(done, tok, place_order(place), bu3, bd3, where)
    done = [*part, tok, order, bu3, bd3, where]

    dense_near, dy = after(done, jnp.concatenate(part, axis=0), dy)
    other = place.core(dense_near)
    dy_mine, dy_z, dy_other = across(dy), place.zp(dy), place.core(dy)
    dense, tailt = dense_in_order(place, dense_near, other, order, share)
    saved, act_x, act_z, act_c = [], [], [], []
    saved.append(run_forward(tok, dense, tailt, 0, experts))
    done = [saved[0][3], dy_other]

    for h in halves[1:]:
        act, dense_h = after(done, saved[-1][3], dense)
        act_x.append(across(act))
        act_z.append(place.zp(act))
        act_c.append(place.core(act))
        saved.append(run_forward(tok, dense_h, tailt, h, experts))
        done = [*act_x[-1], act_z[-1], act_c[-1], saved[-1][3], dy_z, *dy_mine]

    act, far_dy, *rest = after(done, saved[-1][3], dy_z, *act_x[0][1:], *dy_mine[1:])
    dy_near = both_cores(dy_mine, [dy_other, *[place.core(v) for v in rest[nx - 1 :]]])
    rest = rest[: nx - 1]
    act_x.append(across(act))
    act_z.append(place.zp(act))
    act_c.append(place.core(act))
    dy_far = across(far_dy)
    near = both_cores(act_x[0], [act_c[0], *[place.core(v) for v in rest]])
    visit = lambda h, near: [
        run_experts(place, h, list(zip(near, dy_near))[at : at + 4], w_up, bu3, w_down, bd3, experts, slots)
        for at in range(0, len(near), 4)
    ]
    results = [visit(0, near)]
    done = [*act_x[-1], *act_z, act_c[-1], *dy_far]
    done += [r[0] for r in results[0]]

    n_far = len(dy_far)
    vals = after(done, *dy_far, *act_z, *act_x[1][1:], *[r[1] for r in results[0]])
    dy_far = both_cores(vals[:n_far], [place.core(v) for v in vals[:n_far]])
    far = [across(v) for v in vals[n_far : n_far + 2]]
    rest = vals[n_far + 2 :]
    near = both_cores(act_x[1], [act_c[1], *[place.core(v) for v in rest[: nx - 1]]])
    back = [[place.core(v) for v in rest[nx - 1 :]]]
    results.append(visit(1, near))
    done = [*dy_far, *[v for f in far for v in f], *back[0], *[r[0] for r in results[1]]]

    add = lambda a, b: (a.astype(F32) + b.astype(F32)).astype(BF)
    pairs_of = lambda h: [
        p[k] for p in [add(r[0], b) for r, b in zip(results[h], back[h])] for k in range(p.shape[0])
    ]
    home = lambda p: [p[0]] + [place.xs(p[k], nx - k) for k in range(1, nx)]
    n_all = 2 * n_far
    vals = after(done, *[v for f in far for v in f], *[r[1] for r in results[1]])
    far = [vals[:n_far], vals[n_far:n_all]]
    far = [both_cores(f, [place.core(v) for v in f]) for f in far]
    back.append([place.core(v) for v in vals[n_all : n_all + len(results[1])]])
    xs, gs = [[r[k] for rs in results for r in rs] for k in (2, 3)]
    for h in halves:
        src = list(zip(far[h], dy_far))
        for at in range(0, len(src), 4):
            x, g = run_pick(place, h, src[at : at + 4], local, experts, slots)
            xs.append(x)
            gs.append(g)
    for rs in results[:1]:
        near_sent = after(xs[2 * len(rs) :], *[r[0] for r in rs])
        results[0] = [(v, *r[1:]) for v, r in zip(near_sent, rs)]
    backs = [home(pairs_of(0))]
    weights = lambda e, x: run_weight_grad(place, where, e, [x, *xs[1:]], gs, w_up, bu3, w_down)
    tokens_back = lambda i, d, v: run_backward(
        i, v, d, dense, tailt, saved[i // HALF], backs[i // HALF], experts
    )
    sent = weights(0, xs[0])
    done = [*back[1], *sent]

    sent = list(after(done, *sent))
    x, grads, rows_in, *pairs = after(done, xs[0], dy, tok, *pairs_of(1))
    backs.append(home(pairs))
    images, both, level = [], [], None
    wide = dense.shape[1]
    split = share if share % 16 == 0 else 0
    todo = list(range(MICRO))
    for e in range(local):
        crossed = [place.ys(sent[k], k) for k in range(1, ny)]
        done = list(crossed)
        if level is not None:
            moved = [place.zhs(level[k], k) for k in range(1, nh)]
            both.append([level[0], *moved])
            done += moved
        if e + 1 < local:
            later = weights(e + 1, x)
            done += later
        if todo:
            for i in todo[:2]:
                images.append(tokens_back(i, grads, rows_in))
                done += images[-1]
            todo = todo[2:]
        elif e + 1 < local:
            sums = run_dense_grads(place, images, [v[1] for v in saved], wide, split)
            done += sums
        else:
            val = add(sums[0], place.core(sums[1]))
            val = val.reshape(nz, ny, nx, -1, val.shape[1])
            val = stage(jnp.moveaxis(val, 2, 0), nx, place.x, place.xs)
        if e == 0:
            done += backs[0]
        level = functools.reduce(add, [sent[0], *crossed])
        if e + 1 < local:
            x, grads, rows_in, *sent = after(done, xs[0], dy, tok, *later)
        if e == local - 2:
            if not split:
                full = jnp.moveaxis(sums[0].reshape(-1, CORES, share, wide), 1, 0)
                side = lambda c: lax.dynamic_index_in_dim(full, c, 0, keepdims=False)
                sums = [side(c).reshape(-1, wide) for c in (place.c, 1 - place.c)]
            n_tail = used + n_small
            if n_tail > 128:
                sums = [jnp.pad(v, ((0, 0), (0, n_tail - 128))) for v in sums]
            sums = after([*done, level], *sums)

    across_x = val
    moved = [place.zhs(level[k], k) for k in range(1, nh)]
    both.append([level[0], *moved])
    part_b_up = sum(r[4] for rs in results for r in rs).reshape(local, place.nd, -1)
    part_b_down = sum(r[5] for rs in results for r in rs).reshape(local, place.nd, -1)
    small = jnp.concatenate([part_b_up, part_b_down], axis=2).transpose(1, 0, 2)
    small = small.reshape(place.nd, -1)
    small = jnp.pad(small, ((0, 0), (0, share * n_small - small.shape[1])))
    small = small.reshape(nz, ny, share, n_small).astype(BF)
    at = 4 * width + used
    val = jnp.concatenate([val[..., :at], small, val[..., at + n_small :]], axis=-1)
    val = stage(jnp.moveaxis(val, 1, 0), ny, place.y, place.ys)
    pick = lambda i: lax.dynamic_index_in_dim(val, i % nz, 0, keepdims=False)
    parts = [pick(place.z)] + [place.zs(pick(place.z + k), k) for k in range(1, nz)]
    qkv_g, proj_g, router_g, gains_g, biases_g, tiny = split_sum(
        parts, [3 * width, width, experts, 2, 5, n_small]
    )
    stored = []
    for e, b in enumerate(both):
        b = after([qkv_g], *b) if e == local - 1 else b
        stored = store_expert(e, local, b, stored)
    grad_up, grad_down = stored
    outs = after([across_x], *[v[0] for v in images])
    gtoks = after([across_x], *[v[1] for v in images])
    tokens = lambda v: jnp.concatenate(v, axis=0)[:, :SEQ].reshape(-1, width)
    tiny = tiny.reshape(-1)[: local * (hb + width // place.nd)].reshape(local, -1)
    return (
        tokens(outs),
        tokens(gtoks),
        gains_g,
        biases_g,
        qkv_g,
        proj_g,
        router_g,
        grad_up,
        tiny[:, :hb],
        grad_down,
        tiny[:, hb:],
    )


def solution(mesh):
    place = Place(mesh)
    tok = P(("dp", "expert"), None)
    in_specs = (tok,) * 8 + (
        P("expert", None, None),
        P("expert", None),
        P("expert", None, None),
        P("expert", None),
    )
    out_specs = (tok,) * 7 + (
        P("expert", None, "dp"),
        P("expert", "dp"),
        P("expert", "dp", None),
        P("expert", "dp"),
    )

    def run(*args):
        return on_device(place, *args)

    return jax.shard_map(run, mesh=mesh, in_specs=in_specs, out_specs=out_specs, check_vma=False)
```

```python
import functools

import jax
import jax.numpy as jnp
from jax import lax
from jax.experimental import pallas as pl
from jax.experimental.pallas import tpu as pltpu
from jax.sharding import PartitionSpec as P

HEAD = 64
SEQ = 197
MICRO = 4
HALF = 2
CORES = 2
EPSILON = 1e-06
BF = jnp.bfloat16
F32 = jnp.float32


LOW = -1e30


def cost(us):
    return pl.CostEstimate(flops=int(us * 0.35e9), bytes_accessed=1 << 20, transcendentals=0)


def dot(left, right, over_left, over_right):
    return lax.dot_general(
        left, right, (((over_left,), (over_right,)), ((), ())), preferred_element_type=F32
    )


def iota(shape, axis):
    return lax.broadcasted_iota(jnp.int32, shape, axis)


def norm_rows(row_block):
    row_mean = jnp.mean(row_block, axis=-1, keepdims=True)
    centred = row_block - row_mean
    inv_std = lax.rsqrt(jnp.mean(centred * centred, axis=-1, keepdims=True) + EPSILON)
    return (centred * inv_std, inv_std)


def norm_back(grad_h, normed, inv_std, gain_vec):
    scaled = grad_h * gain_vec
    return inv_std * (
        scaled
        - jnp.mean(scaled, axis=-1, keepdims=True)
        - normed * jnp.mean(scaled * normed, axis=-1, keepdims=True)
    )


def gelu_parts(pre_act):
    normal_cdf = 0.5 * (1.0 + lax.erf(pre_act * 0.7071067811865476))
    normal_pdf = jnp.exp(-0.5 * pre_act * pre_act) * 0.3989422804014327
    return (normal_cdf, normal_pdf)


def half_lanes(pair, side):
    lane = iota(pair.shape, 1)
    keep = lane < HEAD if side == 0 else lane >= HEAD
    return jnp.where(keep, pair, jnp.zeros_like(pair))


def router_rows(tailt, act, experts):
    logits = dot(tailt, act, 1, 1)[:experts]
    top = jnp.max(logits, axis=0, keepdims=True)
    powers = jnp.exp(logits - top)
    return powers / jnp.sum(powers, axis=0, keepdims=True)


def forward_kernel(experts, tok, dense, tailt, qkv_o, mix_o, res_o, act_o, lse_o):
    width = tok.shape[2]
    rows = tok.shape[1]
    pairs = width // (2 * HEAD)
    vec = tailt[...].astype(F32)[experts : experts + 7]
    x = tok[0].astype(F32)
    normed, _ = norm_rows(x)
    act = (normed * vec[0:1] + vec[5:6]).astype(BF)
    bias = jnp.concatenate([vec[2:3], jnp.zeros_like(vec[2:3]), vec[3:4]], axis=1)
    qkv_o[0] = (dot(act, dense[:, : 3 * width], 1, 0) + bias).astype(BF)
    seen = iota((rows, rows), 1) < SEQ
    lse_all = jnp.zeros((rows, 128), F32)
    lane = iota((rows, 128), 1)
    for p in range(pairs):
        at = p * 2 * HEAD
        q = qkv_o[0, :, at : at + 2 * HEAD]
        k = qkv_o[0, :, width + at : width + at + 2 * HEAD]
        v = qkv_o[0, :, 2 * width + at : 2 * width + at + 2 * HEAD]
        both = None
        for side in range(2):
            scores = dot(half_lanes(q, side), k, 1, 1) * (HEAD ** (-0.5))
            scores = jnp.where(seen, scores, LOW)
            top = jnp.max(scores, axis=1, keepdims=True)
            lse = top + jnp.log(jnp.sum(jnp.exp(scores - top), axis=1, keepdims=True))
            low = jnp.exp(scores - lse).astype(BF)
            part = dot(low, half_lanes(v, side), 1, 0)
            both = part if both is None else both + part
            lse_all = jnp.where(lane == 2 * p + side, lse, lse_all)
        mix_o[0, :, at : at + 2 * HEAD] = both.astype(BF)
    lse_o[0] = lse_all
    resid = x + (dot(mix_o[0], dense[:, 3 * width : 4 * width], 1, 0) + vec[4:5])
    res_o[0] = resid
    normed, _ = norm_rows(resid)
    act = (normed * vec[1:2] + vec[6:7]).astype(BF)
    act_o[0] = act
    gates = router_rows(tailt[...], act, experts)
    half = experts // 2
    blank = jnp.zeros((half, width // 2 - rows), F32)
    packed = jnp.concatenate([gates[:half], blank, gates[half:], blank], axis=1)
    act_o[0, rows - half :, :] = packed.astype(BF)


def run_forward(tok, dense, tailt, part, experts):
    _, rows, width = tok.shape
    whole = lambda a: pl.BlockSpec(a.shape, lambda i: (0,) * a.ndim)
    row = lambda n: pl.BlockSpec((1, rows, n), lambda i: (i, 0, 0))
    out = lambda n, d: jax.ShapeDtypeStruct((HALF, rows, n), d)
    return pl.pallas_call(
        functools.partial(forward_kernel, experts),
        grid=(HALF,),
        in_specs=[
            pl.BlockSpec((1, rows, width), lambda i: (part * HALF + i, 0, 0)),
            whole(dense),
            whole(tailt),
        ],
        out_specs=[row(3 * width), row(width), row(width), row(width), row(128)],
        out_shape=[out(3 * width, BF), out(width, BF), out(width, F32), out(width, BF), out(128, F32)],
        name="dense_forward",
        cost_estimate=cost(5),
        compiler_params=pltpu.CompilerParams(vmem_limit_bytes=24 << 20),
    )(tok, dense, tailt)


def packed_row(block, experts, e):
    rows, width = block.shape
    half = experts // 2
    table = block[rows - half :].astype(F32)
    side = e // half
    line = jnp.sum(jnp.where(iota(table.shape, 0) == e - side * half, table, 0.0), axis=0, keepdims=True)
    mid = width // 2
    return jnp.where(side == 0, line[:, :rows], line[:, mid : mid + rows])


def pick_rows(experts, local, slots, ei, sources, x_ref, g_ref, raw_ref, gate_ref, p_ref):
    for s, (act, dys) in enumerate(sources):
        for i in range(HALF):
            block = s * HALF + i
            at = block * slots
            rows, dyr = act[i], dys[i]
            hot, gates = [], []
            for j in range(local):
                slot = packed_row(dyr, experts, ei * local + j)
                gate = packed_row(rows, experts, ei * local + j)
                hit = iota((slots, rows.shape[0]), 0).astype(F32) == slot
                gates.append(jnp.sum(jnp.where(hit, gate, 0.0), axis=1, keepdims=True))
                hot.append(jnp.where(hit, 1.0, 0.0).astype(BF))
            hot = jnp.concatenate(hot, axis=0)
            x = dot(hot, rows, 1, 0).astype(BF)
            raw = dot(hot, dyr, 1, 0)
            if p_ref is not None:
                p_ref[block] = hot
            for j in range(local):
                cut = slice(j * slots, (j + 1) * slots)
                x_ref[j, at : at + slots, :] = x[cut]
                g_ref[j, at : at + slots, :] = (gates[j] * raw[cut]).astype(BF)
                if raw_ref is not None:
                    raw_ref[j, at : at + slots, :] = raw[cut].astype(BF)
                    gate_ref[j, at : at + slots, :] = jnp.broadcast_to(gates[j], (slots, 128))


def expert_kernel(experts, n_src, slots, chunk, at_ref, *refs):
    acts, refs = refs[:n_src], refs[n_src:]
    dys, refs = refs[:n_src], refs[n_src:]
    wu, bu, wd, bd = refs[:4]
    out_near, out_far, x_ref, g_ref, gbu, gbd = refs[4:10]
    raw_ref, gate_ref, p_ref, resg_ref, din_ref, dg_ref = refs[10:]
    local = x_ref.shape[0]
    rows = acts[0].shape[1]
    ei = at_ref[0]
    e = pl.program_id(0)

    @pl.when(e == 0)
    def _():
        pick_rows(
            experts, local, slots, ei, list(zip(acts, dys)), x_ref, g_ref, raw_ref, gate_ref, p_ref
        )

    x, g = x_ref[e], g_ref[e]
    res = din = None
    for h in range(0, wu.shape[2], chunk):
        cut = slice(h, h + chunk)
        up, down = wu[0, :, cut], wd[0, cut]
        pre = dot(x, up, 1, 0) + bu[pl.ds(e, 1), cut]
        cdf, pdf = gelu_parts(pre)
        hid = (pre * cdf).astype(BF)
        dpre = (dot(g, down, 1, 1) * (cdf + pre * pdf)).astype(BF)
        gbu[0, :, cut] = jnp.sum(dpre.astype(F32), axis=0, keepdims=True)
        res_part, din_part = dot(hid, down, 1, 0), dot(dpre, up, 1, 1)
        res = res_part if res is None else res + res_part
        din = din_part if din is None else din + din_part
    gbd[0] = jnp.sum(g.astype(F32), axis=0, keepdims=True)
    res = (res + bd[pl.ds(e, 1), :]).astype(BF).astype(F32)
    dg = jnp.sum(res * raw_ref[e].astype(F32), axis=1, keepdims=True)
    dg_ref[e] = jnp.broadcast_to(dg, dg_ref.shape[1:])
    resg_ref[e] = (gate_ref[e][:, 0:1] * res).astype(BF)
    din_ref[e] = din.astype(BF)

    @pl.when(e == local - 1)
    def _():
        for s in range(n_src):
            out = (out_near, out_far)[s % CORES]

            for i in range(HALF):
                block = s * HALF + i
                at = block * slots
                hot = p_ref[block]
                for kind, ref in enumerate((resg_ref, din_ref)):
                    part = jnp.concatenate([ref[j, at : at + slots, :] for j in range(local)], axis=0)
                    to = (kind * HALF + i) * rows
                    out[s // CORES, to : to + rows, :] = dot(hot, part, 0, 0).astype(BF)
                eid = iota((experts, rows), 0)
                dprob = jnp.zeros((experts, rows), F32)
                for j in range(local):
                    dg = dg_ref[j, at : at + slots, :][:, 0:1]
                    mine = hot[j * slots : (j + 1) * slots].astype(F32)
                    row = jnp.sum(mine * dg, axis=0, keepdims=True)
                    dprob = jnp.where(eid == ei * local + j, row, dprob)
                to = 2 * HALF * rows + i * experts
                out[s // CORES, to : to + experts, 0:rows] = dprob.astype(BF)


def run_experts(place, part, sources, w_up, b_up, w_down, b_down, experts, slots):
    local, width, hidden = w_up.shape
    n_src = len(sources)
    span = sources[0][0].shape[1]
    blocks = n_src * HALF
    rows = blocks * slots
    back = HALF * (2 * span + experts)
    flat = [s[i] for i in range(2) for s in sources]
    keep = lambda *s: pl.BlockSpec(s, lambda e, p: (0,) * len(s))
    each = lambda *s: pl.BlockSpec((1,) + s, lambda e, p: (e, 0, 0))
    return pl.pallas_call(
        functools.partial(expert_kernel, experts, n_src, slots, min(hidden, 1024)),
        grid_spec=pltpu.PrefetchScalarGridSpec(
            num_scalar_prefetch=1,
            grid=(local,),
            in_specs=[keep(HALF, span, width)] * n_src
            + [pl.BlockSpec((HALF, span, width), lambda e, p: (part, 0, 0))] * n_src
            + [
                each(width, hidden),
                keep(local, hidden),
                each(hidden, width),
                keep(local, width),
            ],
            out_specs=[
                keep(n_src // CORES, back, width),
                keep(n_src // CORES, back, width),
                keep(local, rows, width),
                keep(local, rows, width),
                each(1, hidden),
                each(1, width),
            ],
            scratch_shapes=[
                pltpu.VMEM((local, rows, width), BF),
                pltpu.VMEM((local, rows, 128), F32),
                pltpu.VMEM((blocks, local * slots, span), BF),
                pltpu.VMEM((local, rows, width), BF),
                pltpu.VMEM((local, rows, width), BF),
                pltpu.VMEM((local, rows, 128), F32),
            ],
        ),
        out_shape=[
            jax.ShapeDtypeStruct((n_src // CORES, back, width), BF),
            jax.ShapeDtypeStruct((n_src // CORES, back, width), BF),
            jax.ShapeDtypeStruct((local, rows, width), BF),
            jax.ShapeDtypeStruct((local, rows, width), BF),
            jax.ShapeDtypeStruct((local, 1, hidden), F32),
            jax.ShapeDtypeStruct((local, 1, width), F32),
        ],
        name="experts",
        cost_estimate=cost(24),
        compiler_params=pltpu.CompilerParams(vmem_limit_bytes=60 << 20),
    )(place.ei.reshape(1), *flat, w_up, b_up, w_down, b_down)


def pick_kernel(experts, n_src, slots, ei_ref, *refs):
    x_ref, g_ref = refs[2 * n_src :]
    sources = list(zip(refs[:n_src], refs[n_src : 2 * n_src]))
    pick_rows(experts, x_ref.shape[0], slots, ei_ref[0], sources, x_ref, g_ref, None, None, None)


def run_pick(place, part, sources, local, experts, slots):
    _, span, width = sources[0][0].shape
    n_src = len(sources)
    rows = n_src * HALF * slots
    flat = [s[i] for i in range(2) for s in sources]
    half = lambda h: pl.BlockSpec((HALF, span, width), lambda i, p: (h, 0, 0))
    keep = pl.BlockSpec((local, rows, width), lambda i, p: (0, 0, 0))
    return pl.pallas_call(
        functools.partial(pick_kernel, experts, n_src, slots),
        grid_spec=pltpu.PrefetchScalarGridSpec(
            num_scalar_prefetch=1,
            grid=(1,),
            in_specs=[half(part)] * (2 * n_src),
            out_specs=[keep] * 2,
        ),
        out_shape=[jax.ShapeDtypeStruct((local, rows, width), BF)] * 2,
        name="pick_rows",
        cost_estimate=cost(1),
        compiler_params=pltpu.CompilerParams(vmem_limit_bytes=32 << 20),
    )(place.ei.reshape(1), *flat)


def weight_grad_kernel(e, n_rows, ny, hb, own_ref, *refs):
    xs, gs = refs[:n_rows], refs[n_rows : 2 * n_rows]
    wu, bu, wd = refs[2 * n_rows : 2 * n_rows + 3]
    outs, total = refs[2 * n_rows + 3 : -1], refs[-1]
    up = down = None
    for x_ref, g_ref in zip(xs, gs):
        x, g = x_ref[0], g_ref[0]
        pre = dot(x, wu[0], 1, 0) + bu[e : e + 1, :]
        cdf, pdf = gelu_parts(pre)
        hid = (pre * cdf).astype(BF)
        dpre = (dot(g, wd[0], 1, 1) * (cdf + pre * pdf)).astype(BF)
        down_part, up_part = dot(hid, g, 0, 0), dot(dpre, x, 0, 0)
        down = down_part if down is None else down + down_part
        up = up_part if up is None else up + up_part
    total[0] = up.astype(BF)
    total[1] = down.astype(BF)
    for k in range(ny):
        at = pl.multiple_of(lax.rem(own_ref[0] + k, ny) * hb, 16)
        outs[k][0] = total[:, pl.ds(at, hb), :]


def run_weight_grad(place, where, e, xs, gs, w_up, b_up, w_down):
    _, width, hidden = w_up.shape
    cols = hidden // place.nz
    nh, ny = place.nh, place.ny
    hb = cols // ny
    row = [pl.BlockSpec((1,) + x.shape[1:], lambda k, p: (e, 0, 0)) for x in xs]
    return pl.pallas_call(
        functools.partial(weight_grad_kernel, e, len(xs), ny, hb),
        grid_spec=pltpu.PrefetchScalarGridSpec(
            num_scalar_prefetch=1,
            grid=(nh,),
            in_specs=row
            + row
            + [
                pl.BlockSpec((1, width, cols), lambda k, p: (e, 0, p[k + 1])),
                pl.BlockSpec((b_up.shape[0], cols), lambda k, p: (0, p[k + 1])),
                pl.BlockSpec((1, cols, width), lambda k, p: (e, p[k + 1], 0)),
            ],
            out_specs=[pl.BlockSpec((1, 2, hb, width), lambda k, p: (k, 0, 0, 0))] * ny,
            scratch_shapes=[pltpu.VMEM((2, cols, width), BF)],
        ),
        out_shape=[jax.ShapeDtypeStruct((nh, 2, hb, width), BF)] * ny,
        name="weight_grad",
        cost_estimate=cost(1),
        compiler_params=pltpu.CompilerParams(vmem_limit_bytes=32 << 20),
    )(where, *xs, *gs, w_up, b_up, w_down)


def backward_kernel(experts, n_back, *refs):
    tok, dy, dense, tailt, qkv, resid, act_two, lse = refs[:8]
    moes, dins, dgs = [refs[8 + k * n_back : 8 + (k + 1) * n_back] for k in range(3)]
    out, gtok, dattn_o, act_o, dqkv, acc_t = refs[8 + 3 * n_back :]
    width = tok.shape[2]
    rows = tok.shape[1]
    pairs = width // (2 * HEAD)
    scale = HEAD ** (-0.5)
    total = lambda parts: functools.reduce(jnp.add, [p[...].astype(F32) for p in parts])
    tail = tailt[...]
    vec = tail.astype(F32)[experts : experts + 7]
    res = resid[0]
    out[0] = (res + total(moes)).astype(BF)
    normed_two, inv_two = norm_rows(res)
    probs = router_rows(tail, act_two[0], experts)
    dprob = total(dgs)[:, 0:rows]
    dlogit = probs * (dprob - jnp.sum(dprob * probs, axis=0, keepdims=True))
    dlogit = jnp.concatenate([dlogit, jnp.zeros((128 - experts, rows), F32)], axis=0).astype(BF)
    dact_two = total(dins) + dot(dlogit, tail, 0, 0)
    dyf = jnp.where(iota((rows, width), 0) < SEQ, dy[0].astype(F32), 0.0)
    dresid = dyf + norm_back(dact_two, normed_two, inv_two, vec[1:2])
    dattn = dresid.astype(BF)
    dattn_o[0] = dattn
    dmixed = dot(dattn, dense[:, 3 * width : 4 * width], 1, 1).astype(BF)
    seen = iota((rows, rows), 1) < SEQ
    for p in range(pairs):
        at = p * 2 * HEAD
        q = qkv[0, :, at : at + 2 * HEAD]
        k = qkv[0, :, width + at : width + at + 2 * HEAD]
        v = qkv[0, :, 2 * width + at : 2 * width + at + 2 * HEAD]
        dm = dmixed[:, at : at + 2 * HEAD]
        dq = dk = dv = None
        for side in range(2):
            q_s, dm_s = half_lanes(q, side), half_lanes(dm, side)
            scores = dot(q_s, k, 1, 1) * scale
            which = 2 * p + side
            weights = jnp.exp(jnp.where(seen, scores, LOW) - lse[0][:, which : which + 1])
            low = weights.astype(BF)
            dv_s = dot(low, dm_s, 0, 0)
            dw = dot(dm_s, v, 1, 1)
            ds = (weights * (dw - jnp.sum(dw * weights, axis=1, keepdims=True))).astype(BF)
            dq_s = dot(ds, half_lanes(k, side), 1, 0)
            dk_s = dot(ds, q_s, 0, 0)
            dq = dq_s if dq is None else dq + dq_s
            dk = dk_s if dk is None else dk + dk_s
            dv = dv_s if dv is None else dv + dv_s
        dqkv[0, :, at : at + 2 * HEAD] = (dq * scale).astype(BF)
        dqkv[0, :, width + at : width + at + 2 * HEAD] = (dk * scale).astype(BF)
        dqkv[0, :, 2 * width + at : 2 * width + at + 2 * HEAD] = dv.astype(BF)
    normed_one, inv_one = norm_rows(tok[0].astype(F32))
    act_one = (normed_one * vec[0:1] + vec[5:6]).astype(BF)
    act_o[0] = act_one
    dact_one = dot(dqkv[0], dense[:, : 3 * width], 1, 1)
    gtok[0] = dresid + norm_back(dact_one, normed_one, inv_one, vec[0:1])
    rowsum = lambda v: jnp.sum(v.astype(F32), axis=0, keepdims=True)
    sums = [
        rowsum(dact_one * normed_one),
        rowsum(dact_two * normed_two),
        rowsum(dqkv[0, :, :width]),
        rowsum(dqkv[0, :, 2 * width :]),
        rowsum(dattn),
        rowsum(dact_one),
        rowsum(dact_two),
    ]
    acc_t[...] = dot(dlogit, act_two[0], 1, 0)
    for i, row in enumerate(sums):
        acc_t[experts + i : experts + i + 1, :] = row


def run_backward(image, tok, dy, dense, tailt, saved, backs, experts):
    _, rows, width = tok.shape
    i = image % HALF
    whole = lambda a: pl.BlockSpec(a.shape, lambda k: (0,) * len(a.shape))
    at = lambda j, n: pl.BlockSpec((1, rows, n), lambda k: (j, 0, 0))
    first = 2 * HALF * rows // experts
    back_specs = (
        [pl.BlockSpec((rows, width), lambda k: (i, 0))] * len(backs)
        + [pl.BlockSpec((rows, width), lambda k: (HALF + i, 0))] * len(backs)
        + [pl.BlockSpec((experts, width), lambda k: (first + i, 0))] * len(backs)
    )
    qkv, _, resid, act, lse = saved
    args = [tok, dy, dense, tailt, qkv, resid, act, lse, *backs, *backs, *backs]
    specs = [at(image, width), at(image, width), whole(dense), whole(tailt)]
    specs += [at(i, 3 * width), at(i, width), at(i, width), at(i, 128)] + back_specs
    out = lambda n, d: jax.ShapeDtypeStruct((1, rows, n), d)
    outs = [out(width, BF), out(width, F32), out(width, BF), out(width, BF), out(3 * width, BF)]
    outs += [jax.ShapeDtypeStruct((128, width), F32)]
    return pl.pallas_call(
        functools.partial(backward_kernel, experts, len(backs)),
        grid=(1,),
        in_specs=specs,
        out_specs=[whole(o) for o in outs],
        out_shape=outs,
        name="dense_backward",
        cost_estimate=cost(1),
        compiler_params=pltpu.CompilerParams(vmem_limit_bytes=24 << 20),
    )(*args)


def dense_grads_kernel(share, core_ref, *refs):
    acts, dqkvs, dattns, tails = [refs[k * MICRO : (k + 1) * MICRO] for k in range(4)]
    mixes = refs[4 * MICRO : 4 * MICRO + MICRO // HALF]
    outs = refs[4 * MICRO + MICRO // HALF :]
    full = outs[-1]
    width = acts[0].shape[2]
    join = lambda parts: jnp.concatenate([p[0] for p in parts], axis=0)
    act, dqkv, dattn = join(acts), join(dqkvs), join(dattns)
    mix = jnp.concatenate([m[i] for m in mixes for i in range(HALF)], axis=0)
    for k in range(3):
        full[:, k * width : (k + 1) * width] = dot(
            act, dqkv[:, k * width : (k + 1) * width], 0, 0
        ).astype(BF)
    full[:, 3 * width : 4 * width] = dot(mix, dattn, 0, 0).astype(BF)
    tail = functools.reduce(jnp.add, [t[...] for t in tails])
    full[:, 4 * width :] = jnp.transpose(tail, (1, 0)).astype(BF)
    if share:
        keep, send = outs[:2]
        core = core_ref[0]

        def body(i, carry):
            to = pl.multiple_of(i * share, 16)
            for ref, side in ((keep, core), (send, 1 - core)):
                at = pl.multiple_of((i * CORES + side) * share, 16)
                ref[pl.ds(to, share), :] = full[pl.ds(at, share), :]
            return carry

        lax.fori_loop(0, width // share // CORES, body, 0)


def run_dense_grads(place, parts, mixes, wide, share):
    width = mixes[0].shape[2]
    args = [p[k] for k in (3, 4, 2, 5) for p in parts] + list(mixes)
    vmem = pl.BlockSpec(memory_space=pltpu.VMEM)
    whole = [jax.ShapeDtypeStruct((width, wide), BF)]
    split = [jax.ShapeDtypeStruct((width // CORES, wide), BF)] * 2
    return pl.pallas_call(
        functools.partial(dense_grads_kernel, share),
        in_specs=[pl.BlockSpec(memory_space=pltpu.SMEM)] + [vmem] * len(args),
        out_specs=[vmem] * len(split if share else whole),
        out_shape=split if share else whole,
        scratch_shapes=[pltpu.VMEM((width, wide), BF)] if share else [],
        name="dense_grads",
        cost_estimate=cost(1),
        compiler_params=pltpu.CompilerParams(vmem_limit_bytes=32 << 20),
    )(place.c.reshape(1), *args)


def store_expert_kernel(n, *refs):
    total = functools.reduce(jnp.add, [r[...].astype(F32) for r in refs[:n]])
    up, down = refs[-2:]
    up[0] = jnp.transpose(total[0], (1, 0))
    down[0] = total[1]


def store_expert(e, local, parts, before):
    _, hb, width = parts[0].shape
    whole = pl.BlockSpec(parts[0].shape, lambda k: (0, 0, 0))
    return pl.pallas_call(
        functools.partial(store_expert_kernel, len(parts)),
        grid=(1,),
        in_specs=[whole] * len(parts) + [pl.BlockSpec(memory_space=pl.ANY)] * len(before),
        out_specs=[
            pl.BlockSpec((1, width, hb), lambda k: (e, 0, 0)),
            pl.BlockSpec((1, hb, width), lambda k: (e, 0, 0)),
        ],
        out_shape=[
            jax.ShapeDtypeStruct((local, width, hb), F32),
            jax.ShapeDtypeStruct((local, hb, width), F32),
        ],
        input_output_aliases={len(parts) + k: k for k in range(len(before))},
        name="store_expert",
        cost_estimate=cost(1),
        compiler_params=pltpu.CompilerParams(vmem_limit_bytes=16 << 20),
    )(*parts, *before)


def split_kernel(n, *refs):
    total = functools.reduce(jnp.add, [r[...].astype(F32) for r in refs[:n]])
    at = 0
    for out in refs[n:]:
        out[...] = total[:, at : at + out.shape[1]]
        at += out.shape[1]


def split_sum(parts, widths):
    vmem = pl.BlockSpec(memory_space=pltpu.VMEM)
    return pl.pallas_call(
        functools.partial(split_kernel, len(parts)),
        in_specs=[vmem] * len(parts),
        out_specs=[vmem] * len(widths),
        out_shape=[jax.ShapeDtypeStruct((parts[0].shape[0], w), F32) for w in widths],
        name="split_sum",
        cost_estimate=cost(1),
        compiler_params=pltpu.CompilerParams(vmem_limit_bytes=16 << 20),
    )(*parts)


def arrange_kernel(n, share, at_ref, near, other, dense, tailt):
    def body(i, carry):
        at = pl.multiple_of(i * share, 16)
        for k, ref in enumerate((near, other)):
            to = pl.multiple_of(at_ref[k * n + i] * share, 16)
            dense[pl.ds(to, share), :] = ref[pl.ds(at, share), :]
        return carry

    lax.fori_loop(0, n, body, 0)
    wide = dense.shape[1]
    tailt[...] = jnp.transpose(dense[:, wide - 128 :].astype(F32), (1, 0)).astype(BF)


def arrange(near, other, order, share):
    n = order.shape[0] // 2
    width, wide = 2 * near.shape[0], near.shape[1]
    vmem = pl.BlockSpec(memory_space=pltpu.VMEM)
    return pl.pallas_call(
        functools.partial(arrange_kernel, n, share),
        in_specs=[pl.BlockSpec(memory_space=pltpu.SMEM), vmem, vmem],
        out_specs=[vmem, vmem],
        out_shape=[
            jax.ShapeDtypeStruct((width, wide), BF),
            jax.ShapeDtypeStruct((128, width), BF),
        ],
        name="arrange",
        compiler_params=pltpu.CompilerParams(vmem_limit_bytes=16 << 20),
        cost_estimate=cost(1),
    )(order, near, other)


class Place:
    def __init__(self, mesh):
        self.ne = mesh.shape["expert"]
        self.nd = mesh.shape["dp"]
        self.nx = self.ne // CORES
        bits = self.nd.bit_length() - 1
        self.ny = 1 << (bits // 2)
        self.nz = self.nd // self.ny
        self.nh = self.nz // 2

    def here(self):
        ei = lax.axis_index("expert")
        di = lax.axis_index("dp")
        self.ei, self.di = ei, di
        self.x, self.c = ei // CORES, ei % CORES
        self.z, self.y = di // self.ny, di % self.ny
        self.zh, self.zl = self.z // 2, self.z % 2

    def core(self, val):
        return lax.ppermute(val, "expert", [(i, i ^ 1) for i in range(self.ne)])

    def xs(self, val, k):
        n, c = self.nx, CORES
        return lax.ppermute(val, "expert", [(i, (i // c + k) % n * c + i % c) for i in range(self.ne)])

    def ys(self, val, k):
        n = self.ny
        return lax.ppermute(val, "dp", [(i, i // n * n + (i + k) % n) for i in range(self.nd)])

    def zs(self, val, k):
        n, m = self.nz, self.ny
        return lax.ppermute(val, "dp", [(i, (i // m + k) % n * m + i % m) for i in range(self.nd)])

    def zp(self, val):
        n, m = self.nz, self.ny
        return lax.ppermute(val, "dp", [(i, (i // m ^ 1) * m + i % m) for i in range(self.nd)])

    def zhs(self, val, k):
        n, m = self.nh, self.ny
        return lax.ppermute(
            val,
            "dp",
            [(i, ((i // m // 2 + k) % n * 2 + i // m % 2) * m + i % m) for i in range(self.nd)],
        )

    def xy(self, val, kx, ky):
        def move(i):
            d, e = i // self.ne, i % self.ne
            d = d // self.ny * self.ny + (d + ky) % self.ny
            e = (e // CORES + kx) % self.nx * CORES + e % CORES
            return d * self.ne + e

        return lax.ppermute(val, ("dp", "expert"), [(i, move(i)) for i in range(self.nd * self.ne)])

    def group(self, val):
        mine = [val] + [self.xs(val, k) for k in range(1, self.nx)]
        other = [self.core(v) for v in mine]
        return [v for pair in zip(mine, other) for v in pair]


def after(deps, *vals):
    return lax.optimization_barrier((*vals, *deps))[: len(vals)]


def place_order(place):
    nz, ny, nx = place.nz, place.ny, place.nx
    order = []
    for c in (place.c, 1 - place.c):
        for ky in range(ny):
            for kx in range(nx):
                for kz in range(nz):
                    dp = (place.z - kz) % nz * ny + (place.y - ky) % ny
                    order.append(dp * place.ne + (place.x - kx) % nx * CORES + c)
    return jnp.stack(order).astype(jnp.int32)


def dense_in_order(place, near, other, order, share):
    if share % 16 == 0:
        return arrange(near, other, order, share)
    wide = near.shape[1]
    full = jnp.concatenate([near, other]).reshape(-1, share, wide)
    dense = jnp.zeros_like(full).at[order].set(full).reshape(-1, wide)
    return dense, dense[:, wide - 128 :].T


def stage(v, n, own, shift, dtype=BF):
    pick = lambda i: lax.dynamic_index_in_dim(v, i % n, 0, keepdims=False)
    total = pick(own).astype(F32)
    for k in range(1, n):
        total = total + shift(pick(own + k), k).astype(F32)
    return total.astype(dtype)


def on_device(
    place,
    tokens_in,
    grad_out,
    routes,
    norm_gains,
    biases,
    w_qkv,
    w_proj,
    w_router,
    w_up,
    b_up,
    w_down,
    b_down,
):
    place.here()
    width = tokens_in.shape[1]
    local, _, hidden = w_up.shape
    experts = local * place.ne
    cap = max(2, (2 * SEQ * 13 + 8 * experts - 1) // (8 * experts))
    slots = -(-cap // 16) * 16
    rows = -(-(SEQ + experts // 2) // 16) * 16
    hb = hidden // place.nd
    nh, ny = place.nh, place.ny
    share = w_qkv.shape[0]
    halves = range(MICRO // HALF)

    n_small = -(-local * (hb + width // place.nd) // share)
    used = experts + 7
    assert used + n_small <= 128 or share % 16
    piece = jnp.concatenate([w_qkv, w_proj, w_router, norm_gains, biases], axis=1)
    piece = jnp.pad(piece, ((0, 0), (0, 4 * width + 128 - piece.shape[1])))

    route_rows = routes.reshape(MICRO, SEQ, 2)
    names = jnp.arange(experts, dtype=jnp.int32)
    sel = jnp.any(route_rows[:, :, :, None] == names, axis=2)
    tri = (jnp.arange(SEQ)[:, None] >= jnp.arange(SEQ)[None, :]).astype(BF)
    pos = jnp.einsum("ts,bse->bet", tri, sel.astype(BF), preferred_element_type=F32)
    pos = jnp.where(sel.transpose(0, 2, 1), pos - 1, -1).astype(BF)
    pos = jnp.pad(pos, ((0, 0), (0, 0), (0, width // 2 - SEQ)), constant_values=-1)
    pos = jnp.concatenate([pos[:, : experts // 2], pos[:, experts // 2 :]], axis=2)

    blocks = lambda v: v.reshape(MICRO, SEQ, width)
    tok = jnp.pad(blocks(tokens_in), ((0, 0), (0, rows - SEQ), (0, 0)))
    gap = jnp.zeros((MICRO, rows - SEQ - experts // 2, width), BF)
    dy = jnp.concatenate([blocks(grad_out), gap, pos], axis=1)
    bu3, bd3 = b_up.astype(F32), b_down.astype(F32)
    across = lambda v: [v] + [place.xs(v, k) for k in range(1, place.nx)]
    both_cores = lambda mine, other: [v for pair in zip(mine, other) for v in pair]
    both_cores = lambda mine, other: [v for pair in zip(mine, other) for v in pair]
    nx, nz = place.nx, place.nz

    line = [piece] + [place.zs(piece, k) for k in range(1, nz)]
    done = line

    (line,) = after(done, jnp.concatenate(line, axis=0))
    moves = [(ky, kx) for ky in range(ny) for kx in range(nx)]
    part = [line] + [place.xy(line, kx, ky) for ky, kx in moves[1:]]
    own = [(place.zh + k) % nh * 2 + place.zl for k in range(nh)]
    where = jnp.stack([place.y, *own]).astype(jnp.int32)
    tok, order, bu3, bd3, where = after(done, tok, place_order(place), bu3, bd3, where)
    done = [*part, tok, order, bu3, bd3, where]

    dense_near, dy = after(done, jnp.concatenate(part, axis=0), dy)
    other = place.core(dense_near)
    dy_mine, dy_z, dy_other = across(dy), place.zp(dy), place.core(dy)
    dense, tailt = dense_in_order(place, dense_near, other, order, share)
    saved, act_x, act_c = [], [], []
    saved.append(run_forward(tok, dense, tailt, 0, experts))
    done = [saved[0][3], dy_other]

    for h in halves[1:]:
        act, dense_h = after(done, saved[-1][3], dense)
        act_x.append(across(act))
        act_c.append(place.core(act))
        saved.append(run_forward(tok, dense_h, tailt, h, experts))
        done = [*act_x[-1], act_c[-1], saved[-1][3], dy_z, *dy_mine]

    act, far_dy, *rest = after(done, saved[-1][3], dy_z, *act_x[0][1:], *dy_mine[1:])
    dy_near = both_cores(dy_mine, [dy_other, *[place.core(v) for v in rest[nx - 1 :]]])
    rest = rest[: nx - 1]
    act_x.append(across(act))
    act_z = place.zp(jnp.concatenate([*[v[0] for v in act_x[:-1]], act], axis=0))
    act_c.append(place.core(act))
    dy_far = across(far_dy)
    near = both_cores(act_x[0], [act_c[0], *[place.core(v) for v in rest]])
    visit = lambda h, near: [
        run_experts(place, h, list(zip(near, dy_near))[at : at + 4], w_up, bu3, w_down, bd3, experts, slots)
        for at in range(0, len(near), 4)
    ]
    results = [visit(0, near)]
    done = [*act_x[-1], act_z, act_c[-1], *dy_far]
    done += [r[0] for r in results[0]]

    n_far = len(dy_far)
    vals = after(done, *dy_far, act_z, *act_x[1][1:], *[r[1] for r in results[0]])
    dy_far = both_cores(vals[:n_far], [place.core(v) for v in vals[:n_far]])
    far = across(vals[n_far])
    rest = vals[n_far + 1 :]
    near = both_cores(act_x[1], [act_c[1], *[place.core(v) for v in rest[: nx - 1]]])
    back = [[place.core(v) for v in rest[nx - 1 :]]]
    results.append(visit(1, near))
    done = [*dy_far, *far, *back[0], *[r[0] for r in results[1]]]

    add = lambda a, b: (a.astype(F32) + b.astype(F32)).astype(BF)
    pairs_of = lambda h: [
        add(r[0][k], b[k]) for r, b in zip(results[h], back[h]) for k in range(b.shape[0])
    ]
    home = lambda p: [p[0]] + [place.xs(p[k], nx - k) for k in range(1, nx)]
    backs = [home(pairs_of(0))]
    vals = after(done, *far, *[r[1] for r in results[1]])
    far = both_cores(vals[:n_far], [place.core(v) for v in vals[:n_far]])
    back.append([place.core(v) for v in vals[n_far:]])
    xs, gs = [[r[k] for rs in results for r in rs] for k in (2, 3)]
    for h in halves:
        src = list(zip(far, dy_far))
        for at in range(0, len(src), 4):
            x, g = run_pick(place, h, src[at : at + 4], local, experts, slots)
            xs.append(x)
            gs.append(g)
    weights = lambda e, x: run_weight_grad(place, where, e, [x, *xs[1:]], gs, w_up, bu3, w_down)
    tokens_back = lambda i, d, v: run_backward(
        i, v, d, dense, tailt, saved[i // HALF], backs[i // HALF], experts
    )
    sent = weights(0, xs[0])
    done = [*back[1], *backs[0], *sent]

    sent = list(after(done, *sent))
    x, grads, rows_in, *pairs = after(done, xs[0], dy, tok, *pairs_of(1))
    backs.append(home(pairs))
    images, both, level = [], [], None
    wide = dense.shape[1]
    split = share if share % 16 == 0 else 0
    todo = list(range(MICRO))
    for e in range(local):
        crossed = [place.ys(sent[k], k) for k in range(1, ny)]
        done = list(crossed)
        if level is not None:
            moved = [place.zhs(level[k], k) for k in range(1, nh)]
            both.append([level[0], *moved])
            done += moved
        if e + 1 < local:
            later = weights(e + 1, x)
            done += later
        if todo:
            for i in todo[:2]:
                images.append(tokens_back(i, grads, rows_in))
                done += images[-1]
            todo = todo[2:]
        elif e + 1 < local:
            sums = run_dense_grads(place, images, [v[1] for v in saved], wide, split)
            done += sums
        else:
            val = add(sums[0], place.core(sums[1]))
            val = val.reshape(nz, ny, nx, -1, val.shape[1])
            val = stage(jnp.moveaxis(val, 2, 0), nx, place.x, place.xs)
        level = functools.reduce(add, [sent[0], *crossed])
        if e + 1 < local:
            x, grads, rows_in, *sent = after(done, xs[0], dy, tok, *later)
        if e == local - 2:
            if not split:
                full = jnp.moveaxis(sums[0].reshape(-1, CORES, share, wide), 1, 0)
                side = lambda c: lax.dynamic_index_in_dim(full, c, 0, keepdims=False)
                sums = [side(c).reshape(-1, wide) for c in (place.c, 1 - place.c)]
            n_tail = used + n_small
            if n_tail > 128:
                sums = [jnp.pad(v, ((0, 0), (0, n_tail - 128))) for v in sums]
            sums = after([*done, level], *sums)

    across_x = val
    moved = [place.zhs(level[k], k) for k in range(1, nh)]
    both.append([level[0], *moved])
    part_b_up = sum(r[4] for rs in results for r in rs).reshape(local, place.nd, -1)
    part_b_down = sum(r[5] for rs in results for r in rs).reshape(local, place.nd, -1)
    small = jnp.concatenate([part_b_up, part_b_down], axis=2).transpose(1, 0, 2)
    small = small.reshape(place.nd, -1)
    small = jnp.pad(small, ((0, 0), (0, share * n_small - small.shape[1])))
    small = small.reshape(nz, ny, share, n_small).astype(BF)
    at = 4 * width + used
    val = jnp.concatenate([val[..., :at], small, val[..., at + n_small :]], axis=-1)
    val = stage(jnp.moveaxis(val, 1, 0), ny, place.y, place.ys)
    pick = lambda i: lax.dynamic_index_in_dim(val, i % nz, 0, keepdims=False)
    parts = [pick(place.z)] + [place.zs(pick(place.z + k), k) for k in range(1, nz)]
    qkv_g, proj_g, router_g, gains_g, biases_g, tiny = split_sum(
        parts, [3 * width, width, experts, 2, 5, n_small]
    )
    stored = []
    for e, b in enumerate(both):
        b = after([qkv_g] if e == local - 1 else [val], *b)
        stored = store_expert(e, local, b, stored)
    grad_up, grad_down = stored
    outs = after([across_x], *[v[0] for v in images])
    gtoks = after([across_x], *[v[1] for v in images])
    tokens = lambda v: jnp.concatenate(v, axis=0)[:, :SEQ].reshape(-1, width)
    tiny = tiny.reshape(-1)[: local * (hb + width // place.nd)].reshape(local, -1)
    return (
        tokens(outs),
        tokens(gtoks),
        gains_g,
        biases_g,
        qkv_g,
        proj_g,
        router_g,
        grad_up,
        tiny[:, :hb],
        grad_down,
        tiny[:, hb:],
    )


def solution(mesh):
    place = Place(mesh)
    tok = P(("dp", "expert"), None)
    in_specs = (tok,) * 8 + (
        P("expert", None, None),
        P("expert", None),
        P("expert", None, None),
        P("expert", None),
    )
    out_specs = (tok,) * 7 + (
        P("expert", None, "dp"),
        P("expert", "dp"),
        P("expert", "dp", None),
        P("expert", "dp"),
    )

    def run(*args):
        return on_device(place, *args)

    return jax.shard_map(run, mesh=mesh, in_specs=in_specs, out_specs=out_specs, check_vma=False)
```

```python
import functools

import jax
import jax.numpy as jnp
from jax import lax
from jax.experimental import pallas as pl
from jax.experimental.pallas import tpu as pltpu
from jax.sharding import PartitionSpec as P

HEAD = 64
SEQ = 197
MICRO = 4
HALF = 2
CORES = 2
EPSILON = 1e-06
BF = jnp.bfloat16
F32 = jnp.float32


LOW = -1e30


def cost(us):
    return pl.CostEstimate(flops=int(us * 0.35e9), bytes_accessed=1 << 20, transcendentals=0)


def dot(left, right, over_left, over_right):
    return lax.dot_general(
        left, right, (((over_left,), (over_right,)), ((), ())), preferred_element_type=F32
    )


def iota(shape, axis):
    return lax.broadcasted_iota(jnp.int32, shape, axis)


def norm_rows(row_block):
    row_mean = jnp.mean(row_block, axis=-1, keepdims=True)
    centred = row_block - row_mean
    inv_std = lax.rsqrt(jnp.mean(centred * centred, axis=-1, keepdims=True) + EPSILON)
    return (centred * inv_std, inv_std)


def norm_back(grad_h, normed, inv_std, gain_vec):
    scaled = grad_h * gain_vec
    return inv_std * (
        scaled
        - jnp.mean(scaled, axis=-1, keepdims=True)
        - normed * jnp.mean(scaled * normed, axis=-1, keepdims=True)
    )


def gelu_parts(pre_act):
    normal_cdf = 0.5 * (1.0 + lax.erf(pre_act * 0.7071067811865476))
    normal_pdf = jnp.exp(-0.5 * pre_act * pre_act) * 0.3989422804014327
    return (normal_cdf, normal_pdf)


def half_lanes(pair, side):
    lane = iota(pair.shape, 1)
    keep = lane < HEAD if side == 0 else lane >= HEAD
    return jnp.where(keep, pair, jnp.zeros_like(pair))


def router_rows(tailt, act, experts):
    logits = dot(tailt, act, 1, 1)[:experts]
    top = jnp.max(logits, axis=0, keepdims=True)
    powers = jnp.exp(logits - top)
    return powers / jnp.sum(powers, axis=0, keepdims=True)


def forward_kernel(experts, tok, dense, tailt, qkv_o, mix_o, res_o, act_o, lse_o):
    width = tok.shape[2]
    rows = tok.shape[1]
    pairs = width // (2 * HEAD)
    vec = tailt[...].astype(F32)[experts : experts + 7]
    x = tok[0].astype(F32)
    normed, _ = norm_rows(x)
    act = (normed * vec[0:1] + vec[5:6]).astype(BF)
    bias = jnp.concatenate([vec[2:3], jnp.zeros_like(vec[2:3]), vec[3:4]], axis=1)
    qkv_o[0] = (dot(act, dense[:, : 3 * width], 1, 0) + bias).astype(BF)
    seen = iota((rows, rows), 1) < SEQ
    lse_all = jnp.zeros((rows, 128), F32)
    lane = iota((rows, 128), 1)
    for p in range(pairs):
        at = p * 2 * HEAD
        q = qkv_o[0, :, at : at + 2 * HEAD]
        k = qkv_o[0, :, width + at : width + at + 2 * HEAD]
        v = qkv_o[0, :, 2 * width + at : 2 * width + at + 2 * HEAD]
        both = None
        for side in range(2):
            scores = dot(half_lanes(q, side), k, 1, 1) * (HEAD ** (-0.5))
            scores = jnp.where(seen, scores, LOW)
            top = jnp.max(scores, axis=1, keepdims=True)
            lse = top + jnp.log(jnp.sum(jnp.exp(scores - top), axis=1, keepdims=True))
            low = jnp.exp(scores - lse).astype(BF)
            part = dot(low, half_lanes(v, side), 1, 0)
            both = part if both is None else both + part
            lse_all = jnp.where(lane == 2 * p + side, lse, lse_all)
        mix_o[0, :, at : at + 2 * HEAD] = both.astype(BF)
    lse_o[0] = lse_all
    resid = x + (dot(mix_o[0], dense[:, 3 * width : 4 * width], 1, 0) + vec[4:5])
    res_o[0] = resid
    normed, _ = norm_rows(resid)
    act = (normed * vec[1:2] + vec[6:7]).astype(BF)
    act_o[0] = act
    gates = router_rows(tailt[...], act, experts)
    half = experts // 2
    blank = jnp.zeros((half, width // 2 - rows), F32)
    packed = jnp.concatenate([gates[:half], blank, gates[half:], blank], axis=1)
    act_o[0, rows - half :, :] = packed.astype(BF)


def run_forward(tok, dense, tailt, part, experts):
    _, rows, width = tok.shape
    whole = lambda a: pl.BlockSpec(a.shape, lambda i: (0,) * a.ndim)
    row = lambda n: pl.BlockSpec((1, rows, n), lambda i: (i, 0, 0))
    out = lambda n, d: jax.ShapeDtypeStruct((HALF, rows, n), d)
    return pl.pallas_call(
        functools.partial(forward_kernel, experts),
        grid=(HALF,),
        in_specs=[
            pl.BlockSpec((1, rows, width), lambda i: (part * HALF + i, 0, 0)),
            whole(dense),
            whole(tailt),
        ],
        out_specs=[row(3 * width), row(width), row(width), row(width), row(128)],
        out_shape=[out(3 * width, BF), out(width, BF), out(width, F32), out(width, BF), out(128, F32)],
        name="dense_forward",
        cost_estimate=cost(5),
        compiler_params=pltpu.CompilerParams(vmem_limit_bytes=24 << 20),
    )(tok, dense, tailt)


def packed_row(block, experts, e):
    rows, width = block.shape
    half = experts // 2
    table = block[rows - half :].astype(F32)
    side = e // half
    line = jnp.sum(jnp.where(iota(table.shape, 0) == e - side * half, table, 0.0), axis=0, keepdims=True)
    mid = width // 2
    return jnp.where(side == 0, line[:, :rows], line[:, mid : mid + rows])


def pick_rows(experts, local, slots, ei, sources, x_ref, g_ref, raw_ref, gate_ref, p_ref):
    for s, (act, dys) in enumerate(sources):
        for i in range(HALF):
            block = s * HALF + i
            at = block * slots
            rows, dyr = act[i], dys[i]
            hot, gates = [], []
            for j in range(local):
                slot = packed_row(dyr, experts, ei * local + j)
                gate = packed_row(rows, experts, ei * local + j)
                hit = iota((slots, rows.shape[0]), 0).astype(F32) == slot
                gates.append(jnp.sum(jnp.where(hit, gate, 0.0), axis=1, keepdims=True))
                hot.append(jnp.where(hit, 1.0, 0.0).astype(BF))
            hot = jnp.concatenate(hot, axis=0)
            x = dot(hot, rows, 1, 0).astype(BF)
            raw = dot(hot, dyr, 1, 0)
            if p_ref is not None:
                p_ref[block] = hot
            for j in range(local):
                cut = slice(j * slots, (j + 1) * slots)
                x_ref[j, at : at + slots, :] = x[cut]
                g_ref[j, at : at + slots, :] = (gates[j] * raw[cut]).astype(BF)
                if raw_ref is not None:
                    raw_ref[j, at : at + slots, :] = raw[cut].astype(BF)
                    gate_ref[j, at : at + slots, :] = jnp.broadcast_to(gates[j], (slots, 128))


def expert_kernel(experts, n_src, slots, chunk, at_ref, *refs):
    acts, refs = refs[:n_src], refs[n_src:]
    dys, refs = refs[:n_src], refs[n_src:]
    wu, bu, wd, bd = refs[:4]
    out_near, out_far, x_ref, g_ref, gbu, gbd = refs[4:10]
    raw_ref, gate_ref, p_ref, resg_ref, din_ref, dg_ref = refs[10:]
    local = x_ref.shape[0]
    rows = acts[0].shape[1]
    ei = at_ref[0]
    e = pl.program_id(0)

    @pl.when(e == 0)
    def _():
        pick_rows(
            experts, local, slots, ei, list(zip(acts, dys)), x_ref, g_ref, raw_ref, gate_ref, p_ref
        )

    x, g = x_ref[e], g_ref[e]
    res = din = None
    for h in range(0, wu.shape[2], chunk):
        cut = slice(h, h + chunk)
        up, down = wu[0, :, cut], wd[0, cut]
        pre = dot(x, up, 1, 0) + bu[pl.ds(e, 1), cut]
        cdf, pdf = gelu_parts(pre)
        hid = (pre * cdf).astype(BF)
        dpre = (dot(g, down, 1, 1) * (cdf + pre * pdf)).astype(BF)
        gbu[0, :, cut] = jnp.sum(dpre.astype(F32), axis=0, keepdims=True)
        res_part, din_part = dot(hid, down, 1, 0), dot(dpre, up, 1, 1)
        res = res_part if res is None else res + res_part
        din = din_part if din is None else din + din_part
    gbd[0] = jnp.sum(g.astype(F32), axis=0, keepdims=True)
    res = (res + bd[pl.ds(e, 1), :]).astype(BF).astype(F32)
    dg = jnp.sum(res * raw_ref[e].astype(F32), axis=1, keepdims=True)
    dg_ref[e] = jnp.broadcast_to(dg, dg_ref.shape[1:])
    resg_ref[e] = (gate_ref[e][:, 0:1] * res).astype(BF)
    din_ref[e] = din.astype(BF)

    @pl.when(e == local - 1)
    def _():
        for s in range(n_src):
            out = (out_near, out_far)[s % CORES]

            for i in range(HALF):
                block = s * HALF + i
                at = block * slots
                hot = p_ref[block]
                for kind, ref in enumerate((resg_ref, din_ref)):
                    part = jnp.concatenate([ref[j, at : at + slots, :] for j in range(local)], axis=0)
                    to = (kind * HALF + i) * rows
                    out[s // CORES, to : to + rows, :] = dot(hot, part, 0, 0).astype(BF)
                eid = iota((experts, rows), 0)
                dprob = jnp.zeros((experts, rows), F32)
                for j in range(local):
                    dg = dg_ref[j, at : at + slots, :][:, 0:1]
                    mine = hot[j * slots : (j + 1) * slots].astype(F32)
                    row = jnp.sum(mine * dg, axis=0, keepdims=True)
                    dprob = jnp.where(eid == ei * local + j, row, dprob)
                to = 2 * HALF * rows + i * experts
                out[s // CORES, to : to + experts, 0:rows] = dprob.astype(BF)


def half_spec(a, part):
    at = part if a.shape[0] > HALF else 0
    return pl.BlockSpec((HALF, *a.shape[1:]), lambda e, p: (at, 0, 0))


def run_experts(place, part, sources, w_up, b_up, w_down, b_down, experts, slots):
    local, width, hidden = w_up.shape
    n_src = len(sources)
    span = sources[0][0].shape[1]
    blocks = n_src * HALF
    rows = blocks * slots
    back = HALF * (2 * span + experts)
    flat = [s[i] for i in range(2) for s in sources]
    keep = lambda *s: pl.BlockSpec(s, lambda e, p: (0,) * len(s))
    half = lambda a: half_spec(a, part)
    each = lambda *s: pl.BlockSpec((1,) + s, lambda e, p: (e, 0, 0))
    return pl.pallas_call(
        functools.partial(expert_kernel, experts, n_src, slots, min(hidden, 1024)),
        grid_spec=pltpu.PrefetchScalarGridSpec(
            num_scalar_prefetch=1,
            grid=(local,),
            in_specs=[half(a) for a in flat]
            + [
                each(width, hidden),
                keep(local, hidden),
                each(hidden, width),
                keep(local, width),
            ],
            out_specs=[
                keep(n_src // CORES, back, width),
                keep(n_src // CORES, back, width),
                keep(local, rows, width),
                keep(local, rows, width),
                each(1, hidden),
                each(1, width),
            ],
            scratch_shapes=[
                pltpu.VMEM((local, rows, width), BF),
                pltpu.VMEM((local, rows, 128), F32),
                pltpu.VMEM((blocks, local * slots, span), BF),
                pltpu.VMEM((local, rows, width), BF),
                pltpu.VMEM((local, rows, width), BF),
                pltpu.VMEM((local, rows, 128), F32),
            ],
        ),
        out_shape=[
            jax.ShapeDtypeStruct((n_src // CORES, back, width), BF),
            jax.ShapeDtypeStruct((n_src // CORES, back, width), BF),
            jax.ShapeDtypeStruct((local, rows, width), BF),
            jax.ShapeDtypeStruct((local, rows, width), BF),
            jax.ShapeDtypeStruct((local, 1, hidden), F32),
            jax.ShapeDtypeStruct((local, 1, width), F32),
        ],
        name="experts",
        cost_estimate=cost(24),
        compiler_params=pltpu.CompilerParams(vmem_limit_bytes=50 << 20),
    )(place.ei.reshape(1), *flat, w_up, b_up, w_down, b_down)


def pick_kernel(experts, n_src, slots, ei_ref, *refs):
    x_ref, g_ref = refs[2 * n_src :]
    sources = list(zip(refs[:n_src], refs[n_src : 2 * n_src]))
    pick_rows(experts, x_ref.shape[0], slots, ei_ref[0], sources, x_ref, g_ref, None, None, None)


def run_pick(place, part, sources, local, experts, slots):
    _, span, width = sources[0][0].shape
    n_src = len(sources)
    rows = n_src * HALF * slots
    flat = [s[i] for i in range(2) for s in sources]
    keep = pl.BlockSpec((local, rows, width), lambda i, p: (0, 0, 0))
    return pl.pallas_call(
        functools.partial(pick_kernel, experts, n_src, slots),
        grid_spec=pltpu.PrefetchScalarGridSpec(
            num_scalar_prefetch=1,
            grid=(1,),
            in_specs=[half_spec(a, part) for a in flat],
            out_specs=[keep] * 2,
        ),
        out_shape=[jax.ShapeDtypeStruct((local, rows, width), BF)] * 2,
        name="pick_rows",
        cost_estimate=cost(1),
        compiler_params=pltpu.CompilerParams(vmem_limit_bytes=32 << 20),
    )(place.ei.reshape(1), *flat)


def weight_grad_kernel(e, n_rows, ny, hb, own_ref, *refs):
    xs, gs = refs[:n_rows], refs[n_rows : 2 * n_rows]
    wu, bu, wd = refs[2 * n_rows : 2 * n_rows + 3]
    outs, total = refs[2 * n_rows + 3 : -1], refs[-1]
    up = down = None
    for x_ref, g_ref in zip(xs, gs):
        x, g = x_ref[0], g_ref[0]
        pre = dot(x, wu[0], 1, 0) + bu[e : e + 1, :]
        cdf, pdf = gelu_parts(pre)
        hid = (pre * cdf).astype(BF)
        dpre = (dot(g, wd[0], 1, 1) * (cdf + pre * pdf)).astype(BF)
        down_part, up_part = dot(hid, g, 0, 0), dot(dpre, x, 0, 0)
        down = down_part if down is None else down + down_part
        up = up_part if up is None else up + up_part
    total[0] = up.astype(BF)
    total[1] = down.astype(BF)
    for k in range(ny):
        at = pl.multiple_of(lax.rem(own_ref[0] + k, ny) * hb, 16)
        outs[k][0] = total[:, pl.ds(at, hb), :]


def run_weight_grad(place, where, e, xs, gs, w_up, b_up, w_down):
    _, width, hidden = w_up.shape
    cols = hidden // place.nz
    nh, ny = place.nh, place.ny
    hb = cols // ny
    row = [pl.BlockSpec((1,) + x.shape[1:], lambda k, p: (e, 0, 0)) for x in xs]
    return pl.pallas_call(
        functools.partial(weight_grad_kernel, e, len(xs), ny, hb),
        grid_spec=pltpu.PrefetchScalarGridSpec(
            num_scalar_prefetch=1,
            grid=(nh,),
            in_specs=row
            + row
            + [
                pl.BlockSpec((1, width, cols), lambda k, p: (e, 0, p[k + 1])),
                pl.BlockSpec((b_up.shape[0], cols), lambda k, p: (0, p[k + 1])),
                pl.BlockSpec((1, cols, width), lambda k, p: (e, p[k + 1], 0)),
            ],
            out_specs=[pl.BlockSpec((1, 2, hb, width), lambda k, p: (k, 0, 0, 0))] * ny,
            scratch_shapes=[pltpu.VMEM((2, cols, width), BF)],
        ),
        out_shape=[jax.ShapeDtypeStruct((nh, 2, hb, width), BF)] * ny,
        name="weight_grad",
        cost_estimate=cost(1),
        compiler_params=pltpu.CompilerParams(vmem_limit_bytes=32 << 20),
    )(where, *xs, *gs, w_up, b_up, w_down)


def backward_kernel(experts, n_back, *refs):
    tok, dy, dense, tailt, qkv, resid, act_two, lse = refs[:8]
    moes, dins, dgs = [refs[8 + k * n_back : 8 + (k + 1) * n_back] for k in range(3)]
    out, gtok, dattn_o, act_o, dqkv, acc_t = refs[8 + 3 * n_back :]
    width = tok.shape[2]
    rows = tok.shape[1]
    pairs = width // (2 * HEAD)
    scale = HEAD ** (-0.5)
    total = lambda parts: functools.reduce(jnp.add, [p[...].astype(F32) for p in parts])
    tail = tailt[...]
    vec = tail.astype(F32)[experts : experts + 7]
    res = resid[0]
    out[0] = (res + total(moes)).astype(BF)
    normed_two, inv_two = norm_rows(res)
    probs = router_rows(tail, act_two[0], experts)
    dprob = total(dgs)[:, 0:rows]
    dlogit = probs * (dprob - jnp.sum(dprob * probs, axis=0, keepdims=True))
    dlogit = jnp.concatenate([dlogit, jnp.zeros((128 - experts, rows), F32)], axis=0).astype(BF)
    dact_two = total(dins) + dot(dlogit, tail, 0, 0)
    dyf = jnp.where(iota((rows, width), 0) < SEQ, dy[0].astype(F32), 0.0)
    dresid = dyf + norm_back(dact_two, normed_two, inv_two, vec[1:2])
    dattn = dresid.astype(BF)
    dattn_o[0] = dattn
    dmixed = dot(dattn, dense[:, 3 * width : 4 * width], 1, 1).astype(BF)
    seen = iota((rows, rows), 1) < SEQ
    for p in range(pairs):
        at = p * 2 * HEAD
        q = qkv[0, :, at : at + 2 * HEAD]
        k = qkv[0, :, width + at : width + at + 2 * HEAD]
        v = qkv[0, :, 2 * width + at : 2 * width + at + 2 * HEAD]
        dm = dmixed[:, at : at + 2 * HEAD]
        dq = dk = dv = None
        for side in range(2):
            q_s, dm_s = half_lanes(q, side), half_lanes(dm, side)
            scores = dot(q_s, k, 1, 1) * scale
            which = 2 * p + side
            weights = jnp.exp(jnp.where(seen, scores, LOW) - lse[0][:, which : which + 1])
            low = weights.astype(BF)
            dv_s = dot(low, dm_s, 0, 0)
            dw = dot(dm_s, v, 1, 1)
            ds = (weights * (dw - jnp.sum(dw * weights, axis=1, keepdims=True))).astype(BF)
            dq_s = dot(ds, half_lanes(k, side), 1, 0)
            dk_s = dot(ds, q_s, 0, 0)
            dq = dq_s if dq is None else dq + dq_s
            dk = dk_s if dk is None else dk + dk_s
            dv = dv_s if dv is None else dv + dv_s
        dqkv[0, :, at : at + 2 * HEAD] = (dq * scale).astype(BF)
        dqkv[0, :, width + at : width + at + 2 * HEAD] = (dk * scale).astype(BF)
        dqkv[0, :, 2 * width + at : 2 * width + at + 2 * HEAD] = dv.astype(BF)
    normed_one, inv_one = norm_rows(tok[0].astype(F32))
    act_one = (normed_one * vec[0:1] + vec[5:6]).astype(BF)
    act_o[0] = act_one
    dact_one = dot(dqkv[0], dense[:, : 3 * width], 1, 1)
    gtok[0] = dresid + norm_back(dact_one, normed_one, inv_one, vec[0:1])
    rowsum = lambda v: jnp.sum(v.astype(F32), axis=0, keepdims=True)
    sums = [
        rowsum(dact_one * normed_one),
        rowsum(dact_two * normed_two),
        rowsum(dqkv[0, :, :width]),
        rowsum(dqkv[0, :, 2 * width :]),
        rowsum(dattn),
        rowsum(dact_one),
        rowsum(dact_two),
    ]
    acc_t[...] = dot(dlogit, act_two[0], 1, 0)
    for i, row in enumerate(sums):
        acc_t[experts + i : experts + i + 1, :] = row


def run_backward(image, tok, dy, dense, tailt, saved, backs, experts):
    _, rows, width = tok.shape
    i = image % HALF
    whole = lambda a: pl.BlockSpec(a.shape, lambda k: (0,) * len(a.shape))
    at = lambda j, n: pl.BlockSpec((1, rows, n), lambda k: (j, 0, 0))
    first = 2 * HALF * rows // experts
    back_specs = (
        [pl.BlockSpec((rows, width), lambda k: (i, 0))] * len(backs)
        + [pl.BlockSpec((rows, width), lambda k: (HALF + i, 0))] * len(backs)
        + [pl.BlockSpec((experts, width), lambda k: (first + i, 0))] * len(backs)
    )
    qkv, _, resid, act, lse = saved
    args = [tok, dy, dense, tailt, qkv, resid, act, lse, *backs, *backs, *backs]
    specs = [at(image, width), at(image, width), whole(dense), whole(tailt)]
    specs += [at(i, 3 * width), at(i, width), at(i, width), at(i, 128)] + back_specs
    out = lambda n, d: jax.ShapeDtypeStruct((1, rows, n), d)
    outs = [out(width, BF), out(width, F32), out(width, BF), out(width, BF), out(3 * width, BF)]
    outs += [jax.ShapeDtypeStruct((128, width), F32)]
    return pl.pallas_call(
        functools.partial(backward_kernel, experts, len(backs)),
        grid=(1,),
        in_specs=specs,
        out_specs=[whole(o) for o in outs],
        out_shape=outs,
        name="dense_backward",
        cost_estimate=cost(1),
        compiler_params=pltpu.CompilerParams(vmem_limit_bytes=24 << 20),
    )(*args)


def dense_grads_kernel(share, core_ref, *refs):
    acts, dqkvs, dattns, tails = [refs[k * MICRO : (k + 1) * MICRO] for k in range(4)]
    mixes = refs[4 * MICRO : 4 * MICRO + MICRO // HALF]
    outs = refs[4 * MICRO + MICRO // HALF :]
    full = outs[-1]
    width = acts[0].shape[2]
    join = lambda parts: jnp.concatenate([p[0] for p in parts], axis=0)
    act, dqkv, dattn = join(acts), join(dqkvs), join(dattns)
    mix = jnp.concatenate([m[i] for m in mixes for i in range(HALF)], axis=0)
    for k in range(3):
        full[:, k * width : (k + 1) * width] = dot(
            act, dqkv[:, k * width : (k + 1) * width], 0, 0
        ).astype(BF)
    full[:, 3 * width : 4 * width] = dot(mix, dattn, 0, 0).astype(BF)
    tail = functools.reduce(jnp.add, [t[...] for t in tails])
    full[:, 4 * width :] = jnp.transpose(tail, (1, 0)).astype(BF)
    if share:
        keep, send = outs[:2]
        core = core_ref[0]

        def body(i, carry):
            to = pl.multiple_of(i * share, 16)
            for ref, side in ((keep, core), (send, 1 - core)):
                at = pl.multiple_of((i * CORES + side) * share, 16)
                ref[pl.ds(to, share), :] = full[pl.ds(at, share), :]
            return carry

        lax.fori_loop(0, width // share // CORES, body, 0)


def run_dense_grads(place, parts, mixes, wide, share):
    width = mixes[0].shape[2]
    args = [p[k] for k in (3, 4, 2, 5) for p in parts] + list(mixes)
    vmem = pl.BlockSpec(memory_space=pltpu.VMEM)
    whole = [jax.ShapeDtypeStruct((width, wide), BF)]
    split = [jax.ShapeDtypeStruct((width // CORES, wide), BF)] * 2
    return pl.pallas_call(
        functools.partial(dense_grads_kernel, share),
        in_specs=[pl.BlockSpec(memory_space=pltpu.SMEM)] + [vmem] * len(args),
        out_specs=[vmem] * len(split if share else whole),
        out_shape=split if share else whole,
        scratch_shapes=[pltpu.VMEM((width, wide), BF)] if share else [],
        name="dense_grads",
        cost_estimate=cost(1),
        compiler_params=pltpu.CompilerParams(vmem_limit_bytes=24 << 20),
    )(place.c.reshape(1), *args)


def store_expert_kernel(n, *refs):
    total = functools.reduce(jnp.add, [r[...].astype(F32) for r in refs[:n]])
    up, down = refs[-2:]
    up[0] = jnp.transpose(total[0], (1, 0))
    down[0] = total[1]


def store_expert(e, local, parts, before):
    _, hb, width = parts[0].shape
    whole = pl.BlockSpec(parts[0].shape, lambda k: (0, 0, 0))
    return pl.pallas_call(
        functools.partial(store_expert_kernel, len(parts)),
        grid=(1,),
        in_specs=[whole] * len(parts) + [pl.BlockSpec(memory_space=pl.ANY)] * len(before),
        out_specs=[
            pl.BlockSpec((1, width, hb), lambda k: (e, 0, 0)),
            pl.BlockSpec((1, hb, width), lambda k: (e, 0, 0)),
        ],
        out_shape=[
            jax.ShapeDtypeStruct((local, width, hb), F32),
            jax.ShapeDtypeStruct((local, hb, width), F32),
        ],
        input_output_aliases={len(parts) + k: k for k in range(len(before))},
        name="store_expert",
        cost_estimate=cost(1),
        compiler_params=pltpu.CompilerParams(vmem_limit_bytes=16 << 20),
    )(*parts, *before)


def split_kernel(n, *refs):
    total = functools.reduce(jnp.add, [r[...].astype(F32) for r in refs[:n]])
    at = 0
    for out in refs[n:]:
        out[...] = total[:, at : at + out.shape[1]]
        at += out.shape[1]


def split_sum(parts, widths):
    vmem = pl.BlockSpec(memory_space=pltpu.VMEM)
    return pl.pallas_call(
        functools.partial(split_kernel, len(parts)),
        in_specs=[vmem] * len(parts),
        out_specs=[vmem] * len(widths),
        out_shape=[jax.ShapeDtypeStruct((parts[0].shape[0], w), F32) for w in widths],
        name="split_sum",
        cost_estimate=cost(1),
        compiler_params=pltpu.CompilerParams(vmem_limit_bytes=16 << 20),
    )(*parts)


def arrange_kernel(n, share, at_ref, near, other, dense, tailt):
    def body(i, carry):
        at = pl.multiple_of(i * share, 16)
        for k, ref in enumerate((near, other)):
            to = pl.multiple_of(at_ref[k * n + i] * share, 16)
            dense[pl.ds(to, share), :] = ref[pl.ds(at, share), :]
        return carry

    lax.fori_loop(0, n, body, 0)
    wide = dense.shape[1]
    tailt[...] = jnp.transpose(dense[:, wide - 128 :].astype(F32), (1, 0)).astype(BF)


def arrange(near, other, order, share):
    n = order.shape[0] // 2
    width, wide = 2 * near.shape[0], near.shape[1]
    vmem = pl.BlockSpec(memory_space=pltpu.VMEM)
    return pl.pallas_call(
        functools.partial(arrange_kernel, n, share),
        in_specs=[pl.BlockSpec(memory_space=pltpu.SMEM), vmem, vmem],
        out_specs=[vmem, vmem],
        out_shape=[
            jax.ShapeDtypeStruct((width, wide), BF),
            jax.ShapeDtypeStruct((128, width), BF),
        ],
        name="arrange",
        compiler_params=pltpu.CompilerParams(vmem_limit_bytes=16 << 20),
        cost_estimate=cost(1),
    )(order, near, other)


class Place:
    def __init__(self, mesh):
        self.ne = mesh.shape["expert"]
        self.nd = mesh.shape["dp"]
        self.nx = self.ne // CORES
        bits = self.nd.bit_length() - 1
        self.ny = 1 << (bits // 2)
        self.nz = self.nd // self.ny
        self.nh = self.nz // 2

    def here(self):
        ei = lax.axis_index("expert")
        di = lax.axis_index("dp")
        self.ei, self.di = ei, di
        self.x, self.c = ei // CORES, ei % CORES
        self.z, self.y = di // self.ny, di % self.ny
        self.zh, self.zl = self.z // 2, self.z % 2

    def core(self, val):
        return lax.ppermute(val, "expert", [(i, i ^ 1) for i in range(self.ne)])

    def xs(self, val, k):
        n, c = self.nx, CORES
        return lax.ppermute(val, "expert", [(i, (i // c + k) % n * c + i % c) for i in range(self.ne)])

    def ys(self, val, k):
        n = self.ny
        return lax.ppermute(val, "dp", [(i, i // n * n + (i + k) % n) for i in range(self.nd)])

    def zs(self, val, k):
        n, m = self.nz, self.ny
        return lax.ppermute(val, "dp", [(i, (i // m + k) % n * m + i % m) for i in range(self.nd)])

    def zp(self, val):
        n, m = self.nz, self.ny
        return lax.ppermute(val, "dp", [(i, (i // m ^ 1) * m + i % m) for i in range(self.nd)])

    def zhs(self, val, k):
        n, m = self.nh, self.ny
        return lax.ppermute(
            val,
            "dp",
            [(i, ((i // m // 2 + k) % n * 2 + i // m % 2) * m + i % m) for i in range(self.nd)],
        )

    def xy(self, val, kx, ky):
        def move(i):
            d, e = i // self.ne, i % self.ne
            d = d // self.ny * self.ny + (d + ky) % self.ny
            e = (e // CORES + kx) % self.nx * CORES + e % CORES
            return d * self.ne + e

        return lax.ppermute(val, ("dp", "expert"), [(i, move(i)) for i in range(self.nd * self.ne)])

    def group(self, val):
        mine = [val] + [self.xs(val, k) for k in range(1, self.nx)]
        other = [self.core(v) for v in mine]
        return [v for pair in zip(mine, other) for v in pair]


def after(deps, *vals):
    return lax.optimization_barrier((*vals, *deps))[: len(vals)]


def place_order(place):
    nz, ny, nx = place.nz, place.ny, place.nx
    order = []
    for c in (place.c, 1 - place.c):
        for ky in range(ny):
            for kx in range(nx):
                for kz in range(nz):
                    dp = (place.z - kz) % nz * ny + (place.y - ky) % ny
                    order.append(dp * place.ne + (place.x - kx) % nx * CORES + c)
    return jnp.stack(order).astype(jnp.int32)


def dense_in_order(place, near, other, order, share):
    if share % 16 == 0:
        return arrange(near, other, order, share)
    wide = near.shape[1]
    full = jnp.concatenate([near, other]).reshape(-1, share, wide)
    dense = jnp.zeros_like(full).at[order].set(full).reshape(-1, wide)
    return dense, dense[:, wide - 128 :].T


def stage(v, n, own, shift, dtype=BF):
    pick = lambda i: lax.dynamic_index_in_dim(v, i % n, 0, keepdims=False)
    total = pick(own).astype(F32)
    for k in range(1, n):
        total = total + shift(pick(own + k), k).astype(F32)
    return total.astype(dtype)


def on_device(
    place,
    tokens_in,
    grad_out,
    routes,
    norm_gains,
    biases,
    w_qkv,
    w_proj,
    w_router,
    w_up,
    b_up,
    w_down,
    b_down,
):
    place.here()
    width = tokens_in.shape[1]
    local, _, hidden = w_up.shape
    experts = local * place.ne
    cap = max(2, (2 * SEQ * 13 + 8 * experts - 1) // (8 * experts))
    slots = -(-cap // 16) * 16
    rows = -(-(SEQ + experts // 2) // 16) * 16
    hb = hidden // place.nd
    nh, ny = place.nh, place.ny
    share = w_qkv.shape[0]
    halves = range(MICRO // HALF)

    n_small = -(-local * (hb + width // place.nd) // share)
    used = experts + 7
    assert used + n_small <= 128 or share % 16
    piece = jnp.concatenate([w_qkv, w_proj, w_router, norm_gains, biases], axis=1)
    piece = jnp.pad(piece, ((0, 0), (0, 4 * width + 128 - piece.shape[1])))

    route_rows = routes.reshape(MICRO, SEQ, 2)
    names = jnp.arange(experts, dtype=jnp.int32)
    sel = jnp.any(route_rows[:, :, :, None] == names, axis=2)
    tri = (jnp.arange(SEQ)[:, None] >= jnp.arange(SEQ)[None, :]).astype(BF)
    pos = jnp.einsum("ts,bse->bet", tri, sel.astype(BF), preferred_element_type=F32)
    pos = jnp.where(sel.transpose(0, 2, 1), pos - 1, -1).astype(BF)
    pos = jnp.pad(pos, ((0, 0), (0, 0), (0, width // 2 - SEQ)), constant_values=-1)
    pos = jnp.concatenate([pos[:, : experts // 2], pos[:, experts // 2 :]], axis=2)

    blocks = lambda v: v.reshape(MICRO, SEQ, width)
    tok = jnp.pad(blocks(tokens_in), ((0, 0), (0, rows - SEQ), (0, 0)))
    gap = jnp.zeros((MICRO, rows - SEQ - experts // 2, width), BF)
    dy = jnp.concatenate([blocks(grad_out), gap, pos], axis=1)
    bu3, bd3 = b_up.astype(F32), b_down.astype(F32)
    across = lambda v: [v] + [place.xs(v, k) for k in range(1, place.nx)]
    both_cores = lambda mine, other: [v for pair in zip(mine, other) for v in pair]
    both_cores = lambda mine, other: [v for pair in zip(mine, other) for v in pair]
    nx, nz = place.nx, place.nz

    line = [piece] + [place.zs(piece, k) for k in range(1, nz)]
    done = line

    (line,) = after(done, jnp.concatenate(line, axis=0))
    moves = [(ky, kx) for ky in range(ny) for kx in range(nx)]
    part = [line] + [place.xy(line, kx, ky) for ky, kx in moves[1:]]
    own = [(place.zh + k) % nh * 2 + place.zl for k in range(nh)]
    where = jnp.stack([place.y, *own]).astype(jnp.int32)
    tok, order, bu3, bd3, where = after(done, tok, place_order(place), bu3, bd3, where)
    done = [*part, tok, order, bu3, bd3, where]

    cut = lambda v, h: v[h * HALF : (h + 1) * HALF]
    dense_near, dy, *dys = after(
        done, jnp.concatenate(part, axis=0), dy, *[cut(dy, h) for h in halves]
    )
    other = place.core(dense_near)
    dy_z, dy_other = place.zp(dy), place.core(dy)
    dy_x = [across(dys[0])[1:]]
    dense, tailt = dense_in_order(place, dense_near, other, order, share)
    saved, act_x, act_c = [], [], []
    saved.append(run_forward(tok, dense, tailt, 0, experts))
    done = [saved[0][3], dy_other]

    for h in halves[1:]:
        act, dense_h = after(done, saved[-1][3], dense)
        act_x.append(across(act))
        act_c.append(place.core(act))
        saved.append(run_forward(tok, dense_h, tailt, h, experts))
        done = [*act_x[-1], act_c[-1], saved[-1][3], dy_z, *dy_x[0]]

    act, dy_next, dy_z, *rest = after(
        done, saved[-1][3], dys[1], dy_z, *act_x[0][1:], *dy_x[0]
    )
    dy_all = lambda h, crossed: both_cores(
        [dy, *dy_x[h]], [dy_other, *[place.core(v) for v in crossed]]
    )
    dy_near = [dy_all(0, rest[nx - 1 :])]
    rest = rest[: nx - 1]
    act_x.append(across(act))
    act_z = place.zp(jnp.concatenate([*[v[0] for v in act_x[:-1]], act], axis=0))
    act_c.append(place.core(act))
    dy_x.append(across(dy_next)[1:])
    dz_x = [across(cut(dy_z, 0))[1:]]
    near = both_cores(act_x[0], [act_c[0], *[place.core(v) for v in rest]])
    visit = lambda h, near: [
        run_experts(place, h, list(zip(near, dy_near[h]))[at : at + 4], w_up, bu3, w_down, bd3, experts, slots)
        for at in range(0, len(near), 4)
    ]
    results = [visit(0, near)]
    done = [*act_x[-1], act_z, act_c[-1], *dy_x[1], *dz_x[0]]
    done += [r[0] for r in results[0]]

    n = nx - 1
    far, next_z, *rest = after(
        done, act_z, cut(dy_z, 1), *act_x[1][1:], *dy_x[1], *dz_x[0], *[r[1] for r in results[0]]
    )
    near = both_cores(act_x[1], [act_c[1], *[place.core(v) for v in rest[:n]]])
    dy_near.append(dy_all(1, rest[n : 2 * n]))
    far = across(far)
    dz_x.append(across(next_z)[1:])
    dz_c = [[place.core(v) for v in rest[2 * n : 3 * n]]]
    dz_own = place.core(dy_z)
    back = [[place.core(v) for v in rest[3 * n :]]]
    results.append(visit(1, near))
    done = [dz_own, *dz_x[1], *dz_c[0], *far, *back[0], *[r[0] for r in results[1]]]

    add = lambda a, b: (a.astype(F32) + b.astype(F32)).astype(BF)
    pairs_of = lambda h: [
        add(r[0][k], b[k]) for r, b in zip(results[h], back[h]) for k in range(b.shape[0])
    ]
    home = lambda p: [p[0]] + [place.xs(p[k], nx - k) for k in range(1, nx)]
    backs = [home(pairs_of(0))]
    vals = after(done, *far, *dz_x[1], *[r[1] for r in results[1]])
    far = both_cores(vals[:nx], [place.core(v) for v in vals[:nx]])
    dz_c.append([place.core(v) for v in vals[nx : nx + n]])
    back.append([place.core(v) for v in vals[nx + n :]])
    dy_far = [both_cores([dy_z, *dz_x[h]], [dz_own, *dz_c[h]]) for h in halves]
    xs, gs = [[r[k] for rs in results for r in rs] for k in (2, 3)]
    for h in halves:
        src = list(zip(far, dy_far[h]))
        for at in range(0, len(src), 4):
            x, g = run_pick(place, h, src[at : at + 4], local, experts, slots)
            xs.append(x)
            gs.append(g)
    weights = lambda e, x: run_weight_grad(place, where, e, [x, *xs[1:]], gs, w_up, bu3, w_down)
    tokens_back = lambda i, d, v: run_backward(
        i, v, d, dense, tailt, saved[i // HALF], backs[i // HALF], experts
    )
    sent = weights(0, xs[0])
    done = [*back[1], *backs[0], *sent]

    sent = list(after(done, *sent))
    x, grads, rows_in, *pairs = after(done, xs[0], dy, tok, *pairs_of(1))
    backs.append(home(pairs))
    images, both, level = [], [], None
    wide = dense.shape[1]
    split = share if share % 16 == 0 else 0
    todo = list(range(MICRO))
    for e in range(local):
        crossed = [place.ys(sent[k], k) for k in range(1, ny)]
        done = list(crossed)
        if level is not None:
            moved = [place.zhs(level[k], k) for k in range(1, nh)]
            both.append([level[0], *moved])
            done += moved
        if e + 1 < local:
            later = weights(e + 1, x)
            done += later
        if todo:
            for i in todo[:2]:
                images.append(tokens_back(i, grads, rows_in))
                done += images[-1]
            todo = todo[2:]
        elif e + 1 < local:
            sums = run_dense_grads(place, images, [v[1] for v in saved], wide, split)
            done += sums
        else:
            val = add(sums[0], place.core(sums[1]))
            val = val.reshape(nz, ny, nx, -1, val.shape[1])
            val = stage(jnp.moveaxis(val, 2, 0), nx, place.x, place.xs)
        level = functools.reduce(add, [sent[0], *crossed])
        if e + 1 < local:
            x, grads, rows_in, *sent = after(done, xs[0], dy, tok, *later)
        if e == local - 2:
            if not split:
                full = jnp.moveaxis(sums[0].reshape(-1, CORES, share, wide), 1, 0)
                side = lambda c: lax.dynamic_index_in_dim(full, c, 0, keepdims=False)
                sums = [side(c).reshape(-1, wide) for c in (place.c, 1 - place.c)]
            n_tail = used + n_small
            if n_tail > 128:
                sums = [jnp.pad(v, ((0, 0), (0, n_tail - 128))) for v in sums]
            sums = after([*done, level], *sums)

    across_x = val
    moved = [place.zhs(level[k], k) for k in range(1, nh)]
    both.append([level[0], *moved])
    part_b_up = sum(r[4] for rs in results for r in rs).reshape(local, place.nd, -1)
    part_b_down = sum(r[5] for rs in results for r in rs).reshape(local, place.nd, -1)
    small = jnp.concatenate([part_b_up, part_b_down], axis=2).transpose(1, 0, 2)
    small = small.reshape(place.nd, -1)
    small = jnp.pad(small, ((0, 0), (0, share * n_small - small.shape[1])))
    small = small.reshape(nz, ny, share, n_small).astype(BF)
    at = 4 * width + used
    val = jnp.concatenate([val[..., :at], small, val[..., at + n_small :]], axis=-1)
    val = stage(jnp.moveaxis(val, 1, 0), ny, place.y, place.ys)
    pick = lambda i: lax.dynamic_index_in_dim(val, i % nz, 0, keepdims=False)
    parts = [pick(place.z)] + [place.zs(pick(place.z + k), k) for k in range(1, nz)]
    qkv_g, proj_g, router_g, gains_g, biases_g, tiny = split_sum(
        parts, [3 * width, width, experts, 2, 5, n_small]
    )
    stored = []
    for e, b in enumerate(both):
        b = after([qkv_g] if e == local - 1 else [val], *b)
        stored = store_expert(e, local, b, stored)
    grad_up, grad_down = stored
    outs = after([across_x], *[v[0] for v in images])
    gtoks = after([across_x], *[v[1] for v in images])
    tokens = lambda v: jnp.concatenate(v, axis=0)[:, :SEQ].reshape(-1, width)
    tiny = tiny.reshape(-1)[: local * (hb + width // place.nd)].reshape(local, -1)
    return (
        tokens(outs),
        tokens(gtoks),
        gains_g,
        biases_g,
        qkv_g,
        proj_g,
        router_g,
        grad_up,
        tiny[:, :hb],
        grad_down,
        tiny[:, hb:],
    )


def solution(mesh):
    place = Place(mesh)
    tok = P(("dp", "expert"), None)
    in_specs = (tok,) * 8 + (
        P("expert", None, None),
        P("expert", None),
        P("expert", None, None),
        P("expert", None),
    )
    out_specs = (tok,) * 7 + (
        P("expert", None, "dp"),
        P("expert", "dp"),
        P("expert", "dp", None),
        P("expert", "dp"),
    )

    def run(*args):
        return on_device(place, *args)

    return jax.shard_map(run, mesh=mesh, in_specs=in_specs, out_specs=out_specs, check_vma=False)
```
